32 devices in a mesh: groups: 2 (over x), mp: 16 (over z, y, core).
Axes of the slice: x: 2, y: 2, z: 4, core: 2. Of those that a mesh axis runs over, the one named last changes fastest.
Arguments:
- tokens: bfloat16 [512, 8192], P(('groups', 'mp')), parts along dimension 0, may hold values from -6 to 6
- queries: bfloat16 [512, 8192], P(('groups', 'mp')), parts along dimension 0, may hold values from -35 to 35
- key_proj: bfloat16 [512, 1024], P(('groups', 'mp')), parts along dimension 0, may hold values from -5 to 5
- values: bfloat16 [512, 1024], P(('groups', 'mp')), parts along dimension 0, may hold values from -6 to 6
- seq_lens: int32 [12], P('groups'), parts along dimension 0, may hold values from 21 to 85, as said below
- out_weight: bfloat16 [8192, 8192], P('mp'), may hold values from -0.25 to 0.25
- ffn_gain: float32 [2, 8192], replicated, may hold values from 0.25 to 2.5
- gate_weight: bfloat16 [8192, 12288], P(None, 'mp'), may hold values from -0.0625 to 0.0625
- up_weight: bfloat16 [8192, 12288], P(None, 'mp'), may hold values from -0.0625 to 0.0625
- down_weight: bfloat16 [12288, 8192], P('mp'), may hold values from -0.0546875 to 0.0546875
- slice_table: int32 [96], replicated, may hold values from 0 to 1, as said below
Outputs:
- stream: bfloat16 [512, 8192], P(('groups', 'mp')), parts along dimension 0
- mixed: bfloat16 [512, 8192], P(('groups', 'mp')), parts along dimension 0
The draws below stay inside these ranges and needn't reach their ends.
There are 2 independent parts, one for each index of `groups`. The reference program is written for one: setup_inputs(seed, part) draws one part's arguments, and reference() takes and returns one part's arrays. A program takes and returns all parts, laid end to end along the dimension named above; an argument that names none is the same for every part. Nothing has to cross between parts.
Inputs may be any that keep to these rules, and one draw needn't show every extreme that they name: `seq_lens`: the 6 lengths sum to 256; the shortest is exactly 21 and the longest exactly 85. `slice_table`: exactly 16 entries are 1, the rest 0.
All inputs are finite; a program needn't handle non-finite values.
Results may differ from the reference program's by a relative error of at most 0.02.
Values may be sent and summed in bfloat16 or wider, within the bound.
A program may use at most 128 MiB of HBM per device.

```python
import math
import jax
import jax.numpy as jnp
from jax import lax

D = 8192
QUERY_HEADS = 64
KEY_VALUE_HEADS = 8
HEAD_SIZE = 128
FA = 10240
JOINED = 2
SLICE = 128
SEQS = 6
WINDOW_TOKENS = 256
MIN_LEN = 21
MAX_LEN = 85
UNITS = 12288
SLICES = 96
N_MP = 16


def seq_lengths_from(key):
    base_key = jax.random.fold_in(key, 11)
    first_key, second_key, order_key = jax.random.split(base_key, 3)
    spare = WINDOW_TOKENS - MAX_LEN - 5 * MIN_LEN
    half_one = spare // 2
    half_two = spare - half_one
    cut_one = jax.random.randint(first_key, (), 0, half_one + 1).astype(jnp.int32)
    cut_two = jax.random.randint(second_key, (), 0, half_two + 1).astype(jnp.int32)
    middles = jnp.stack([cut_one, half_one - cut_one, cut_two, half_two - cut_two]).astype(jnp.int32) + MIN_LEN
    pieces = jnp.concatenate([jnp.full((1,), MIN_LEN, jnp.int32), jnp.full((1,), MAX_LEN, jnp.int32), middles])
    order = jax.random.permutation(order_key, SEQS)
    return pieces[order].astype(jnp.int32)


def query_key_pair(key):
    pair_key = jax.random.fold_in(key, 23)
    query_key, keys_random_seed = jax.random.split(pair_key, 2)
    query_out = jnp.clip(jax.random.normal(query_key, (WINDOW_TOKENS, QUERY_HEADS * HEAD_SIZE), jnp.float32), -5.0, 5.0)
    key_result = jnp.clip(jax.random.normal(keys_random_seed, (WINDOW_TOKENS, KEY_VALUE_HEADS * HEAD_SIZE), jnp.float32), -5.0, 5.0)
    return (query_out, key_result)


def draw_seq_lens(key, part):
    return seq_lengths_from(key)


def draw_queries(key, part):
    return query_key_pair(key)[0].astype(jnp.bfloat16)


def draw_key_proj(key, part):
    return query_key_pair(key)[1].astype(jnp.bfloat16)


def draw_slice_table(key, part):
    shuffled = jax.random.permutation(jax.random.fold_in(key, 31), SLICES)
    return (shuffled >= FA // SLICE).astype(jnp.int32)


def block_scale(own_key, dims, shards, least, high):
    def one(axis_at, parts):
        draws = jax.random.uniform(jax.random.fold_in(jax.random.fold_in(own_key, 6), axis_at), (parts,), jnp.float32, least / len(shards), high / len(shards))
        return jnp.repeat(jnp.exp(draws), dims[axis_at] // parts).reshape((-1,) + (1,) * (len(dims) - axis_at - 1))

    gain = one(*shards[0])
    for cut in shards[1:]:
        gain = gain * one(*cut)
    return gain


def gaussian(key, extent, deviation, reach, shards=(), kind=jnp.bfloat16):
    loudness = block_scale(key, extent, shards, -0.22, 0.18) if shards else 1.0
    entries = jax.random.normal(key, extent, jnp.float32) * deviation * loudness
    return jnp.minimum(jnp.maximum(entries, -reach), reach).astype(kind)


def setup_inputs(seed: int = 0, part: int = 0) -> dict:
    key_list = jax.random.split(jax.random.key(seed), 12)
    part_keys = jax.random.split(jax.random.fold_in(key_list[11], part), 12)
    return {
        "tokens": gaussian(part_keys[0], (WINDOW_TOKENS, D), 1.0, 6.0, ((0, 16),)),
        "queries": draw_queries(jax.random.fold_in(jax.random.fold_in(key_list[11], part), 71), part),
        "key_proj": draw_key_proj(jax.random.fold_in(jax.random.fold_in(key_list[11], part), 71), part),
        "values": gaussian(part_keys[3], (WINDOW_TOKENS, KEY_VALUE_HEADS * HEAD_SIZE), 1.0, 6.0, ((0, 16),)),
        "seq_lens": draw_seq_lens(jax.random.fold_in(jax.random.fold_in(key_list[11], part), 71), part),
        "out_weight": gaussian(key_list[5], (QUERY_HEADS * HEAD_SIZE, D), (QUERY_HEADS * HEAD_SIZE // 16) ** -0.5, 0.25, ((0, 16),)),
        "ffn_gain": jnp.clip(jnp.exp(jax.random.uniform(key_list[6], (JOINED, D), jnp.float32, math.log(0.25), math.log(2.5))), 0.25, 2.5),
        "gate_weight": gaussian(key_list[7], (D, UNITS), D ** -0.5, 0.0625, ((1, 16),)),
        "up_weight": gaussian(key_list[8], (D, UNITS), D ** -0.5, 0.0625, ((1, 16),)),
        "down_weight": gaussian(key_list[9], (UNITS, D), UNITS ** -0.5, 0.0546875, ((0, 16),)),
        "slice_table": draw_slice_table(jax.random.fold_in(key_list[11], 71), part),
    }


def reference(tokens, queries, key_proj, values, seq_lens, out_weight, ffn_gain, gate_weight, up_weight, down_weight, slice_table):
    positions = jnp.arange(WINDOW_TOKENS, dtype=jnp.int32)
    seq_ends = jnp.cumsum(seq_lens).astype(jnp.int32)
    segment_ids = lax.optimization_barrier(jnp.sum((positions[:, None] >= seq_ends[None, :]).astype(jnp.int32), axis=1))
    visible = (segment_ids[:, None] == segment_ids[None, :]) & (positions[None, :] <= positions[:, None])
    query_heads_per_group = QUERY_HEADS // KEY_VALUE_HEADS
    score_scale = 1.0 / math.sqrt(HEAD_SIZE)

    def one_head(head):
        query_cols = lax.dynamic_slice_in_dim(queries, (head * HEAD_SIZE).astype(jnp.int32), HEAD_SIZE, 1)
        kv_start = (head // query_heads_per_group * HEAD_SIZE).astype(jnp.int32)
        key_cols = lax.dynamic_slice_in_dim(key_proj, kv_start, HEAD_SIZE, 1)
        value_cols = lax.dynamic_slice_in_dim(values, kv_start, HEAD_SIZE, 1)
        scores = jnp.dot(query_cols, key_cols.T, preferred_element_type=jnp.float32) * score_scale
        masked = jnp.where(visible, scores, -1e+30)
        highest = lax.optimization_barrier(jnp.max(masked, axis=1, keepdims=True))
        expo = jnp.where(visible, jnp.exp(masked - highest), 0.0)
        attn_probs = (expo / lax.optimization_barrier(jnp.sum(expo, axis=1, keepdims=True))).astype(jnp.bfloat16)
        return jnp.dot(attn_probs, value_cols, preferred_element_type=jnp.float32).astype(jnp.bfloat16)
    context = lax.map(one_head, jnp.arange(QUERY_HEADS, dtype=jnp.int32))
    context = jnp.transpose(context, (1, 0, 2)).reshape(WINDOW_TOKENS, QUERY_HEADS * HEAD_SIZE)
    width_dev = QUERY_HEADS * HEAD_SIZE // N_MP

    def attn_group(running, group_idx):
        start_col = (group_idx * width_dev).astype(jnp.int32)
        cols = lax.dynamic_slice_in_dim(context, start_col, width_dev, 1)
        weight_rows = lax.dynamic_slice_in_dim(out_weight, start_col, width_dev, 0)
        term = jnp.dot(cols, weight_rows, preferred_element_type=jnp.float32).astype(jnp.bfloat16)
        term = lax.optimization_barrier(term)
        return (running + term.astype(jnp.float32), None)
    attn_sum, _ = lax.scan(attn_group, jnp.zeros((WINDOW_TOKENS, D), jnp.float32), jnp.arange(N_MP, dtype=jnp.int32))
    stream = (tokens.astype(jnp.float32) + attn_sum).astype(jnp.bfloat16)
    stream_full = stream.astype(jnp.float32)
    inv_rms = lax.rsqrt(lax.optimization_barrier(jnp.mean(stream_full * stream_full, axis=1, keepdims=True)) + 1e-05)
    normed = (stream_full * inv_rms).astype(jnp.bfloat16)
    gate_slices = jnp.transpose(gate_weight.reshape(D, SLICES, SLICE), (1, 0, 2))
    up_slices = jnp.transpose(up_weight.reshape(D, SLICES, SLICE), (1, 0, 2))

    def one_slice(packed):
        ffn_which, gate_cols, up_cols = packed
        gain_row = lax.dynamic_index_in_dim(ffn_gain, ffn_which, 0, keepdims=False)
        slice_input = (normed.astype(jnp.float32) * gain_row[None, :]).astype(jnp.bfloat16)
        gate_val = jnp.dot(slice_input, gate_cols, preferred_element_type=jnp.float32)
        up_val = jnp.dot(slice_input, up_cols, preferred_element_type=jnp.float32)
        return (jax.nn.silu(gate_val) * up_val).astype(jnp.bfloat16)
    hidden = lax.map(one_slice, (slice_table, gate_slices, up_slices))
    slices_dev = SLICES // N_MP
    hidden_groups = jnp.transpose(hidden.reshape(N_MP, slices_dev, WINDOW_TOKENS, SLICE), (0, 2, 1, 3)).reshape(N_MP, WINDOW_TOKENS, slices_dev * SLICE)
    down_groups = down_weight.reshape(N_MP, slices_dev * SLICE, D)

    def ffn_group(running, packed):
        hidden_rows, down_rows = packed
        term = jnp.dot(hidden_rows, down_rows, preferred_element_type=jnp.float32).astype(jnp.bfloat16)
        term = lax.optimization_barrier(term)
        return (running + term.astype(jnp.float32), None)
    ffn_sum, _ = lax.scan(ffn_group, jnp.zeros((WINDOW_TOKENS, D), jnp.float32), (hidden_groups, down_groups))
    mixed = (stream_full + ffn_sum).astype(jnp.bfloat16)
    return (stream, mixed)
```

```python
import functools
import math

import jax
import jax.numpy as jnp
from jax import lax
from jax.experimental import pallas as pl
from jax.experimental.pallas import tpu as pltpu
from jax.sharding import PartitionSpec as P

QUERY_HEADS = 64
HEAD_SIZE = 128
SLICE = 128
CHUNKS = 8
TURN = 4
GAPS = (1, 2, 2, 2, 2, 2, 1)
OWN_GAPS = (1, 3, 3, 3)
MESH = pl.DeviceIdType.MESH
F32 = jnp.float32
BF16 = jnp.bfloat16


def flip(z, zs):
    bits = zs.bit_length() - 1
    out = 0
    for k in range(bits):
        out = out + ((z >> k) & 1) * (1 << (bits - 1 - k))
    return out


def layer_kernel(zs, slices, *refs):
    (seq_lens, table, q_ref, k_ref, v_ref, res_ref, gain_ref, w_hbm, gate_hbm, up_hbm, down_hbm,
     both_ref, packed, got, a_ref, ps, pr, w, gate, up, part, whole, from_core, from_one, from_two, from_z,
     own_core, own_one, own_two, own_z, gained, square, acc, hidden,
     w_sem, gate_sem, up_sem, cs, cr, os, orr, ts, tr, zsend, zrecv, gts, gtr, gos, gor, gcs, gcr,
     rcs, rcr, ros, ror, rts, rtr, rzs, rzr) = refs
    n = w.shape[0]
    half, hw = part.shape[2], part.shape[3]
    rows, cw = 2 * half, 2 * hw
    tok = res_ref.shape[0]
    mp = 4 * zs
    r1, r2 = half // 2, half // 4
    bits = from_z.shape[1]
    q_width = packed.shape[2] - 2 * HEAD_SIZE
    me = lax.axis_index("mp")
    core, y, z = lax.rem(me, 2), lax.rem(me // 2, 2), me // 4
    zr = flip(z, zs)
    near = lax.rem(z, 2)
    own = (y * zs + zr) * tok
    stream_ref, mixed_ref = both_ref.at[0], both_ref.at[1]

    def dev(z_, y_, core_):
        return {"mp": (z_ * 2 + y_) * 2 + core_}

    across_core = dev(z, y, 1 - core)

    def turned(j):
        return jnp.int32(lax.rem(j, TURN) == TURN - 2)

    def order(j):
        t = turned(j)
        b1 = y + t * (near - y)
        b2 = near + t * (y - near)
        flip_y = z * 2 + 1 - y
        flip_z = (z + 1 - 2 * near) * 2 + y
        one = flip_y + t * (flip_z - flip_y)
        two = flip_z + t * (flip_y - flip_z)
        return b1, b2, {"mp": one * 2 + core}, {"mp": two * 2 + core}

    def z_partner(k):
        bit = 2 << k
        up_bit = (z // bit) & 1
        return dev(z + bit * (1 - 2 * up_bit), y, core), up_bit

    def columns(j):
        return pl.ds(pl.multiple_of(j * cw, cw), cw)

    def half_columns(j, c):
        return pl.ds(pl.multiple_of(j * cw + c * hw, hw), hw)

    def span(start, size):
        return pl.ds(pl.multiple_of(start, tok), size)

    def w_copy(j, first):
        src = w_hbm if first else down_hbm
        dst = w.at[j, pl.ds(0, src.shape[0])]
        return pltpu.make_async_copy(src.at[:, columns(j)], dst, w_sem.at[j])

    def gate_copy(j):
        return pltpu.make_async_copy(gate_hbm.at[columns(j), :], gate.at[j], gate_sem.at[j])

    def up_copy(j):
        return pltpu.make_async_copy(up_hbm.at[columns(j), :], up.at[j], up_sem.at[j])

    def remote(src, dst, s, r, to):
        return pltpu.make_async_remote_copy(
            src_ref=src, dst_ref=dst, send_sem=s, recv_sem=r, device_id=to, device_id_type=MESH
        )

    def core_copy(u):
        return remote(part.at[u, 1 - core], from_core.at[u], cs.at[u], cr.at[u], across_core)

    def one_copy(u):
        b1, _, to, _ = order(lax.rem(u, n))
        return remote(part.at[u, core, span((1 - b1) * r1, r1)], from_one.at[u], os.at[u], orr.at[u], to)

    def two_copy(u):
        b1, b2, _, to = order(lax.rem(u, n))
        src = part.at[u, core, span(b1 * r1 + (1 - b2) * r2, r2)]
        return remote(src, from_two.at[u], ts.at[u], tr.at[u], to)

    def z_copy(u, k):
        b1, b2, _, _ = order(lax.rem(u, n))
        src = part.at[u, core, span(b1 * r1 + b2 * r2, r2)]
        return remote(src, from_z.at[u, k], zsend.at[u, k], zrecv.at[u, k], z_partner(k)[0])

    def gtwo_copy(u):
        b1, b2, _, to = order(lax.rem(u, n))
        mine = whole.at[u, core, span(b1 * r1 + b2 * r2, r2)]
        return remote(mine, mine, gts.at[u], gtr.at[u], to)

    def gone_copy(u):
        b1, _, to, _ = order(lax.rem(u, n))
        mine = whole.at[u, core, span(b1 * r1, r1)]
        return remote(mine, mine, gos.at[u], gor.at[u], to)

    def gc_copy(u):
        mine = whole.at[u, core]
        return remote(mine, mine, gcs.at[u], gcr.at[u], across_core)

    def own_core_copy(u):
        j = lax.rem(u, n)
        return remote(part.at[u], own_core.at[j], rcs.at[j], rcr.at[j], across_core)

    def own_one_copy(u):
        j = lax.rem(u, n)
        b1, _, to, _ = order(j)
        src = part.at[u, :, span((1 - b1) * r1, r1)]
        return remote(src, own_one.at[j], ros.at[j], ror.at[j], to)

    def own_two_copy(u):
        j = lax.rem(u, n)
        b1, b2, _, to = order(j)
        src = part.at[u, :, span(b1 * r1 + (1 - b2) * r2, r2)]
        return remote(src, own_two.at[j], rts.at[j], rtr.at[j], to)

    def z_start(j, k):
        b1, b2, _, _ = order(j)
        start = b1 * r1 + b2 * r2
        for i in range(k):
            start = start + z_partner(i)[1] * (r2 >> (i + 1))
        return start

    def own_z_copy(u, k):
        j = lax.rem(u, n)
        to, up_bit = z_partner(k)
        size = r2 >> (k + 1)
        src = part.at[u, :, span(z_start(j, k) + (1 - up_bit) * size, size)]
        return remote(src, own_z.at[j, k, :, pl.ds(0, size)], rzs.at[j, k], rzr.at[j, k], to)

    def head_copy(d):
        to = lax.rem(me + d, mp)
        return remote(packed.at[to], got.at[core, y, zr], ps.at[d], pr.at[d], {"mp": to})

    barrier = pltpu.get_barrier_semaphore()

    @pl.loop(1, mp)
    def _(d):
        pl.semaphore_signal(
            barrier, inc=1, device_id={"mp": lax.rem(me + d, mp)}, device_id_type=MESH
        )

    heads_kv = k_ref.shape[1] // HEAD_SIZE
    per_group = QUERY_HEADS // heads_kv
    local_heads = q_width // HEAD_SIZE
    for to in range(mp):
        head = to * local_heads // per_group
        cols = slice(head * HEAD_SIZE, (head + 1) * HEAD_SIZE)
        packed[to, :, :q_width] = q_ref[:, to * q_width : (to + 1) * q_width]
        packed[to, :, q_width : q_width + HEAD_SIZE] = k_ref[:, cols]
        packed[to, :, q_width + HEAD_SIZE :] = v_ref[:, cols]
    got[core, y, zr] = packed[me]
    pl.semaphore_wait(barrier, mp - 1)

    @pl.loop(1, mp)
    def _(d):
        head_copy(d).start()

    @pl.loop(0, n)
    def _(j):
        w_copy(j, True).start()

    @pl.loop(0, n)
    def _(j):
        gate_copy(j).start()
        up_copy(j).start()

    def position(at):
        token, block = at & (tok - 1), at // tok
        z_at = flip(block & (zs - 1), zs)
        y_at, core_at = (block // zs) & 1, block // (zs * 2)
        return ((z_at * 2 + y_at) * 2 + core_at) * tok + token

    query_pos = position(lax.broadcasted_iota(jnp.int32, (rows, 1), 0))
    key_pos = position(lax.broadcasted_iota(jnp.int32, (1, rows), 1))
    begin = jnp.zeros((rows, 1), jnp.int32)
    end = 0
    for k in range(seq_lens.shape[0]):
        end = end + seq_lens[k]
        begin = jnp.where(query_pos >= end, end, begin)
    visible = (key_pos >= begin) & (key_pos <= query_pos)

    @pl.loop(1, mp)
    def _(d):
        head_copy(d).wait_recv()

    keys = got[:, :, :, :, q_width : q_width + HEAD_SIZE].reshape(rows, HEAD_SIZE)
    vals = got[:, :, :, :, q_width + HEAD_SIZE :].reshape(rows, HEAD_SIZE)
    for h in range(local_heads):
        cols = slice(h * HEAD_SIZE, (h + 1) * HEAD_SIZE)
        heads = got[:, :, :, :, cols].reshape(rows, HEAD_SIZE)
        scores = lax.dot_general(
            heads, keys, (((1,), (1,)), ((), ())), preferred_element_type=F32
        ) * (1.0 / math.sqrt(HEAD_SIZE))
        masked = jnp.where(visible, scores, -1e30)
        highest = jnp.max(masked, axis=1, keepdims=True)
        expo = jnp.where(visible, jnp.exp(masked - highest), 0.0)
        probs = (expo / jnp.sum(expo, axis=1, keepdims=True)).astype(BF16)
        a_ref[:, cols] = jnp.dot(probs, vals, preferred_element_type=F32).astype(BF16)

    @pl.loop(1, mp)
    def _(d):
        head_copy(d).wait_send()

    square[...] = jnp.zeros_like(square)
    acc[...] = jnp.zeros_like(acc)

    def multiply(u):
        t, j = u // n, lax.rem(u, n)

        @pl.when(t == 0)
        def _():
            w_copy(j, True).wait()

        lhs = a_ref[pl.ds(pl.multiple_of(t * half, half), half), :]
        res = jnp.dot(lhs, w[j, : lhs.shape[1], :], preferred_element_type=F32).astype(BF16)
        part[u, 0] = res[:, :hw]
        part[u, 1] = res[:, hw:]

        @pl.when(t == core)
        def _():
            for c in range(2):
                mine = part[u, c, span(own, tok), :].astype(F32) + res_ref[:, half_columns(j, c)].astype(F32)
                part[u, c, span(own, tok), :] = mine.astype(BF16)

        core_copy(u).start()

        @pl.when(t == 1)
        def _():
            w_copy(j, False).start()

    def add_core(u):
        core_copy(u).wait_recv()
        part[u, core] = (part[u, core].astype(F32) + from_core[u].astype(F32)).astype(BF16)
        one_copy(u).start()

    def add_one(u):
        b1, _, _, _ = order(lax.rem(u, n))
        one_copy(u).wait_recv()
        at = span(b1 * r1, r1)
        part[u, core, at, :] = (part[u, core, at, :].astype(F32) + from_one[u].astype(F32)).astype(BF16)
        two_copy(u).start()

    def add_two(u):
        b1, b2, _, _ = order(lax.rem(u, n))
        two_copy(u).wait_recv()
        at = span(b1 * r1 + b2 * r2, r2)
        part[u, core, at, :] = (part[u, core, at, :].astype(F32) + from_two[u].astype(F32)).astype(BF16)
        z_copy(u, 0).start()

    def add_z(u, k):
        b1, b2, _, _ = order(lax.rem(u, n))
        at = span(b1 * r1 + b2 * r2, r2)
        z_copy(u, k).wait_recv()
        total = (part[u, core, at, :].astype(F32) + from_z[u, k].astype(F32)).astype(BF16)
        if k < bits - 1:
            z_copy(u, k).wait_send()
            part[u, core, at, :] = total
            z_copy(u, k + 1).start()
        else:
            whole[u, core, at, :] = total
            gtwo_copy(u).start()

    def spread_one(u):
        gtwo_copy(u).wait_recv()
        gone_copy(u).start()

    def spread_core(u):
        gone_copy(u).wait_recv()
        gc_copy(u).start()

    def consume(u):
        t, j = u // n, lax.rem(u, n)
        gc_copy(u).wait_recv()

        @pl.when(t == 0)
        def _():
            gate_copy(j).wait()
            up_copy(j).wait()

        @pl.when(t == core)
        def _():
            for c in range(2):
                stream_ref[:, half_columns(j, c)] = whole[u, c, span(own, tok), :]

        total = square[...]
        for c in range(2):
            x = whole[u, c].astype(F32)
            for k in range(0, hw, 128):
                total += x[:, k : k + 128] * x[:, k : k + 128]
            for f in range(gained.shape[0]):
                gained[f, :, c * hw : (c + 1) * hw] = (x * gain_ref[f : f + 1, half_columns(j, c)]).astype(BF16)
        square[...] = total
        for s in range(slices):
            cols = slice(s * SLICE, (s + 1) * SLICE)
            both = jnp.concatenate([gate[j, :, cols], up[j, :, cols]], axis=1)
            acc[s] += jnp.dot(gained[table[me * slices + s]], both, preferred_element_type=F32)

        @pl.when(j == n - 1)
        def _():
            inv = lax.rsqrt(jnp.sum(square[...], axis=1, keepdims=True) / (n * cw) + 1e-05)
            for s in range(slices):
                both = acc[s] * inv
                g, u_ = both[:, :SLICE], both[:, SLICE:]
                hidden[t, :, s * SLICE : (s + 1) * SLICE] = (g / (1.0 + jnp.exp(-g)) * u_).astype(BF16)
            square[...] = jnp.zeros_like(square)
            acc[...] = jnp.zeros_like(acc)

    def multiply_down(u):
        t, j = u // n, lax.rem(u, n)
        core_copy(u).wait_send()
        one_copy(u).wait_send()
        two_copy(u).wait_send()
        z_copy(u, bits - 1).wait_send()

        @pl.when(t == 0)
        def _():
            w_copy(j, False).wait()

        lhs = hidden[t]
        res = jnp.dot(lhs, w[j, : lhs.shape[1], :], preferred_element_type=F32).astype(BF16)
        other = turned(j)
        for a in range(2):
            for b in range(2):
                at = span((a * 2 + b + other * (b - a)) * r2, r2)
                for c in range(2):
                    part[u, c, at, :] = res[(a * 2 + b) * r2 : (a * 2 + b + 1) * r2, c * hw : (c + 1) * hw]

        @pl.when(t != core)
        def _():
            own_core_copy(u).start()

    def mine_only(stage):
        def body(u):
            @pl.when(u // n == core)
            def _():
                stage(u)
        return body

    def own_add_core(u):
        j = lax.rem(u, n)
        own_core_copy(u).wait_recv()
        part[u] = (part[u].astype(F32) + own_core[j].astype(F32)).astype(BF16)
        own_one_copy(u).start()

    def own_add_one(u):
        j = lax.rem(u, n)
        b1, _, _, _ = order(j)
        own_one_copy(u).wait_recv()
        at = span(b1 * r1, r1)
        part[u, :, at, :] = (part[u, :, at, :].astype(F32) + own_one[j].astype(F32)).astype(BF16)
        own_two_copy(u).start()

    def own_add_two(u):
        j = lax.rem(u, n)
        own_two_copy(u).wait_recv()
        at = span(z_start(j, 0), r2)
        part[u, :, at, :] = (part[u, :, at, :].astype(F32) + own_two[j].astype(F32)).astype(BF16)
        own_z_copy(u, 0).start()

    def own_add_z(u, k):
        j = lax.rem(u, n)
        size = r2 >> (k + 1)
        own_z_copy(u, k).wait_recv()
        at = span(z_start(j, k + 1), size)
        total = part[u, :, at, :].astype(F32) + own_z[j, k, :, :size].astype(F32)
        if k < bits - 1:
            part[u, :, at, :] = total.astype(BF16)
            own_z_copy(u, k + 1).start()
        else:
            for c in range(2):
                cols = half_columns(j, c)
                mixed_ref[:, cols] = (stream_ref[:, cols].astype(F32) + total[c]).astype(BF16)

    def run(stages, last):
        @pl.loop(0, last)
        def _(i):
            for lag, stage in stages:
                @pl.when((i >= lag) & (i < 2 * n + lag))
                def _(stage=stage, lag=lag):
                    stage(i - lag)

    first = [(0, multiply)]
    lag = 0
    for gap, stage in zip(GAPS, [add_core, add_one, add_two]):
        lag += gap
        first.append((lag, stage))
    for k in range(bits):
        lag += GAPS[3]
        first.append((lag, functools.partial(add_z, k=k)))
    for gap, stage in zip(GAPS[4:], [spread_one, spread_core, consume]):
        lag += gap
        first.append((lag, stage))
    lag += n
    second = [(lag, multiply_down)]
    for gap, stage in zip(OWN_GAPS, [own_add_core, own_add_one, own_add_two]):
        lag += gap
        second.append((lag, mine_only(stage)))
    for k in range(bits):
        lag += OWN_GAPS[3]
        second.append((lag, mine_only(functools.partial(own_add_z, k=k))))
    run((first + second)[::-1], 2 * n + lag)

    @pl.loop(0, 2 * n)
    def _(u):
        gtwo_copy(u).wait_send()
        gone_copy(u).wait_send()
        gc_copy(u).wait_send()

        @pl.when(u // n != core)
        def _():
            own_core_copy(u).wait_send()

        @pl.when(u // n == core)
        def _():
            own_one_copy(u).wait_send()
            own_two_copy(u).wait_send()
            for k in range(bits):
                own_z_copy(u, k).wait_send()


def layer(seq_lens, table, queries, keys, vals, tokens, gain, out_weight, gate_weight, up_weight,
          down_weight, zs):
    tok, width = tokens.shape
    depth = out_weight.shape[0]
    mp = 4 * zs
    rows = tok * mp
    assert tok & (tok - 1) == 0 and zs & (zs - 1) == 0 and zs >= 4
    units = down_weight.shape[0]
    slices = units // SLICE
    n, cw, half = CHUNKS, width // CHUNKS, rows // 2
    hw = cw // 2
    bits = zs.bit_length() - 2
    dma = pltpu.SemaphoreType.DMA
    vmem = pl.BlockSpec(memory_space=pltpu.VMEM)
    hbm = pl.BlockSpec(memory_space=pl.ANY)
    m = 2 * n
    return pl.pallas_call(
        functools.partial(layer_kernel, zs, slices),
        out_shape=jax.ShapeDtypeStruct((2, tok, width), BF16),
        in_specs=[pl.BlockSpec(memory_space=pltpu.SMEM)] * 2 + [vmem] * 5 + [hbm] * 4,
        out_specs=vmem,
        scratch_shapes=[
            pltpu.VMEM((mp, tok, depth + 2 * HEAD_SIZE), BF16),
            pltpu.VMEM((2, 2, zs, tok, depth + 2 * HEAD_SIZE), BF16),
            pltpu.VMEM((rows, depth), BF16),
            dma((mp,)), dma((mp,)),
            pltpu.VMEM((n, max(depth, units), cw), BF16),
            pltpu.VMEM((n, cw, units), BF16),
            pltpu.VMEM((n, cw, units), BF16),
            pltpu.VMEM((m, 2, half, hw), BF16),
            pltpu.VMEM((m, 2, half, hw), BF16),
            pltpu.VMEM((m, half, hw), BF16),
            pltpu.VMEM((m, half // 2, hw), BF16),
            pltpu.VMEM((m, half // 4, hw), BF16),
            pltpu.VMEM((m, bits, half // 4, hw), BF16),
            pltpu.VMEM((n, 2, half, hw), BF16),
            pltpu.VMEM((n, 2, half // 2, hw), BF16),
            pltpu.VMEM((n, 2, half // 4, hw), BF16),
            pltpu.VMEM((n, bits, 2, half // 8, hw), BF16),
            pltpu.VMEM((gain.shape[0], half, cw), BF16),
            pltpu.VMEM((half, 128), F32),
            pltpu.VMEM((slices, half, 2 * SLICE), F32),
            pltpu.VMEM((2, half, units), BF16),
            dma((n,)), dma((n,)), dma((n,)),
            dma((m,)), dma((m,)), dma((m,)), dma((m,)), dma((m,)), dma((m,)), dma((m, bits)), dma((m, bits)),
            dma((m,)), dma((m,)), dma((m,)), dma((m,)), dma((m,)), dma((m,)),
            dma((n,)), dma((n,)), dma((n,)), dma((n,)), dma((n,)), dma((n,)), dma((n, bits)), dma((n, bits)),
        ],
        compiler_params=pltpu.CompilerParams(
            collective_id=0, has_side_effects=True, vmem_limit_bytes=62 << 20
        ),
        name="layer",
    )(seq_lens, table, queries, keys, vals, tokens, gain, out_weight, gate_weight, up_weight, down_weight)


def local(tokens, queries, key_proj, values, seq_lens, out_weight, ffn_gain, gate_weight, up_weight,
          down_weight, slice_table):
    both = layer(
        seq_lens, slice_table, queries, key_proj, values, tokens, ffn_gain, out_weight, gate_weight,
        up_weight, down_weight, lax.axis_size("mp") // 4
    )
    stream, mixed = both[0], both[1]
    return (stream, mixed)


def solution(mesh):
    placed = (
        P(("groups", "mp"), None),
        P(("groups", "mp"), None),
        P(("groups", "mp"), None),
        P(("groups", "mp"), None),
        P("groups"),
        P("mp", None),
        P(),
        P(None, "mp"),
        P(None, "mp"),
        P("mp", None),
        P(),
    )
    return jax.shard_map(
        local,
        mesh=mesh,
        in_specs=placed,
        out_specs=(P(("groups", "mp"), None), P(("groups", "mp"), None)),
        check_vma=False,
    )
```

```python
import functools
import math

import jax
import jax.numpy as jnp
from jax import lax
from jax.experimental import pallas as pl
from jax.experimental.pallas import tpu as pltpu
from jax.sharding import PartitionSpec as P

QUERY_HEADS = 64
HEAD_SIZE = 128
SLICE = 128
CHUNKS = 8
TURN = 4
GAPS = (2, 4, 3, 3, 3, 4, 2)
OWN_GAPS = (1, 4, 4, 4)
SECOND = 4
MESH = pl.DeviceIdType.MESH
F32 = jnp.float32
BF16 = jnp.bfloat16


def flip(z, zs):
    bits = zs.bit_length() - 1
    out = 0
    for k in range(bits):
        out = out + ((z >> k) & 1) * (1 << (bits - 1 - k))
    return out


def layer_kernel(zs, slices, *refs):
    (seq_lens, table, q_ref, k_ref, v_ref, res_ref, gain_ref, w_hbm, gate_hbm, up_hbm, down_hbm,
     both_ref, packed, got, got_kv, a_ref, ps, pr, ks, kr, ws, wr, self_sem, w, gate, up, part, whole, from_core, from_one, from_two, from_z,
     own_core, own_one, own_two, own_z, gained, square, acc, hidden,
     w_sem, gate_sem, up_sem, cs, cr, os, orr, ts, tr, zsend, zrecv, gts, gtr, gos, gor, gcs, gcr,
     rcs, rcr, ros, ror, rts, rtr, rzs, rzr) = refs
    n = w.shape[0]
    half, hw = part.shape[2], part.shape[3]
    rows, cw = 2 * half, 2 * hw
    tok = res_ref.shape[0]
    mp = 4 * zs
    r1, r2 = half // 2, half // 4
    bits = from_z.shape[1]
    q_width = got.shape[4]
    me = lax.axis_index("mp")
    core, y, z = lax.rem(me, 2), lax.rem(me // 2, 2), me // 4
    zr = flip(z, zs)
    near = lax.rem(z, 2)
    own = (y * zs + zr) * tok
    stream_ref, mixed_ref = both_ref.at[0], both_ref.at[1]

    def dev(z_, y_, core_):
        return {"mp": (z_ * 2 + y_) * 2 + core_}

    across_core = dev(z, y, 1 - core)

    def turned(j):
        return jnp.int32(lax.rem(j, TURN) == TURN - 2)

    def order(j):
        t = turned(j)
        b1 = y + t * (near - y)
        b2 = near + t * (y - near)
        flip_y = z * 2 + 1 - y
        flip_z = (z + 1 - 2 * near) * 2 + y
        one = flip_y + t * (flip_z - flip_y)
        two = flip_z + t * (flip_y - flip_z)
        return b1, b2, {"mp": one * 2 + core}, {"mp": two * 2 + core}

    def z_partner(k):
        bit = 2 << k
        up_bit = (z // bit) & 1
        return dev(z + bit * (1 - 2 * up_bit), y, core), up_bit

    def columns(j):
        return pl.ds(pl.multiple_of(j * cw, cw), cw)

    def half_columns(j, c):
        return pl.ds(pl.multiple_of(j * cw + c * hw, hw), hw)

    def span(start, size):
        return pl.ds(pl.multiple_of(start, tok), size)

    def w_copy(j, first):
        src = w_hbm if first else down_hbm
        dst = w.at[j, pl.ds(0, src.shape[0])]
        return pltpu.make_async_copy(src.at[:, columns(j)], dst, w_sem.at[j])

    def gate_copy(j):
        return pltpu.make_async_copy(gate_hbm.at[columns(j), :], gate.at[j], gate_sem.at[j])

    def up_copy(j):
        return pltpu.make_async_copy(up_hbm.at[columns(j), :], up.at[j], up_sem.at[j])

    def remote(src, dst, s, r, to):
        return pltpu.make_async_remote_copy(
            src_ref=src, dst_ref=dst, send_sem=s, recv_sem=r, device_id=to, device_id_type=MESH
        )

    def core_copy(u):
        return remote(part.at[u, 1 - core], from_core.at[u], cs.at[u], cr.at[u], across_core)

    def one_copy(u):
        b1, _, to, _ = order(lax.rem(u, n))
        return remote(part.at[u, core, span((1 - b1) * r1, r1)], from_one.at[u], os.at[u], orr.at[u], to)

    def two_copy(u):
        b1, b2, _, to = order(lax.rem(u, n))
        src = part.at[u, core, span(b1 * r1 + (1 - b2) * r2, r2)]
        return remote(src, from_two.at[u], ts.at[u], tr.at[u], to)

    def z_copy(u, k):
        b1, b2, _, _ = order(lax.rem(u, n))
        src = part.at[u, core, span(b1 * r1 + b2 * r2, r2)]
        return remote(src, from_z.at[u, k], zsend.at[u, k], zrecv.at[u, k], z_partner(k)[0])

    def gtwo_copy(u):
        b1, b2, _, to = order(lax.rem(u, n))
        mine = whole.at[u, core, span(b1 * r1 + b2 * r2, r2)]
        return remote(mine, mine, gts.at[u], gtr.at[u], to)

    def gone_copy(u):
        b1, _, to, _ = order(lax.rem(u, n))
        mine = whole.at[u, core, span(b1 * r1, r1)]
        return remote(mine, mine, gos.at[u], gor.at[u], to)

    def gc_copy(u):
        mine = whole.at[u, core]
        return remote(mine, mine, gcs.at[u], gcr.at[u], across_core)

    def own_core_copy(u):
        j = lax.rem(u, n)
        return remote(part.at[u], own_core.at[j], rcs.at[j], rcr.at[j], across_core)

    def own_one_copy(u):
        j = lax.rem(u, n)
        b1, _, to, _ = order(j)
        src = part.at[u, :, span((1 - b1) * r1, r1)]
        return remote(src, own_one.at[j], ros.at[j], ror.at[j], to)

    def own_two_copy(u):
        j = lax.rem(u, n)
        b1, b2, _, to = order(j)
        src = part.at[u, :, span(b1 * r1 + (1 - b2) * r2, r2)]
        return remote(src, own_two.at[j], rts.at[j], rtr.at[j], to)

    def z_start(j, k):
        b1, b2, _, _ = order(j)
        start = b1 * r1 + b2 * r2
        for i in range(k):
            start = start + z_partner(i)[1] * (r2 >> (i + 1))
        return start

    def own_z_copy(u, k):
        j = lax.rem(u, n)
        to, up_bit = z_partner(k)
        size = r2 >> (k + 1)
        src = part.at[u, :, span(z_start(j, k) + (1 - up_bit) * size, size)]
        return remote(src, own_z.at[j, k, :, pl.ds(0, size)], rzs.at[j, k], rzr.at[j, k], to)

    def q_columns(to):
        return pl.ds(pl.multiple_of(to * q_width, q_width), q_width)

    def q_copy(d):
        to = lax.rem(me + d, mp)
        return remote(q_ref.at[:, q_columns(to)], got.at[core, y, zr], ps.at[d], pr.at[d], {"mp": to})

    def kv_copy(d):
        to = lax.rem(me + d, mp)
        return remote(packed.at[to], got_kv.at[lax.rem(to, 2), core, y, zr], ks.at[d], kr.at[d], {"mp": to})

    def kv_swap():
        mine = got_kv.at[core]
        return remote(mine, mine, ws.at[0], wr.at[0], across_core)

    own_q = pltpu.make_async_copy(q_ref.at[:, q_columns(me)], got.at[core, y, zr], self_sem.at[0])
    own_kv = pltpu.make_async_copy(packed.at[me], got_kv.at[core, core, y, zr], self_sem.at[1])

    barrier = pltpu.get_barrier_semaphore()

    @pl.loop(1, mp)
    def _(d):
        pl.semaphore_signal(
            barrier, inc=1, device_id={"mp": lax.rem(me + d, mp)}, device_id_type=MESH
        )

    @pl.loop(0, n)
    def _(j):
        w_copy(j, True).start()

    @pl.loop(0, n)
    def _(j):
        gate_copy(j).start()
        up_copy(j).start()

    heads_kv = k_ref.shape[1] // HEAD_SIZE
    per_group = QUERY_HEADS // heads_kv
    local_heads = q_width // HEAD_SIZE
    assert per_group % (2 * local_heads) == 0
    for to in range(mp):
        head = to * local_heads // per_group
        cols = slice(head * HEAD_SIZE, (head + 1) * HEAD_SIZE)
        packed[to] = (v_ref if to % 2 else k_ref)[:, cols]
    own_q.start()
    own_kv.start()

    def position(at):
        token, block = at & (tok - 1), at // tok
        z_at = flip(block & (zs - 1), zs)
        y_at, core_at = (block // zs) & 1, block // (zs * 2)
        return ((z_at * 2 + y_at) * 2 + core_at) * tok + token

    def send_queries():
        @pl.loop(1, mp)
        def _(d):
            q_copy(d).start()

    def from_half(t, act):
        @pl.loop(1, mp)
        def _(d):
            @pl.when(lax.rem(me + d, 2) == t)
            def _():
                act(d)

    def attend(t):
        from_half(t, lambda d: q_copy(d).wait_recv())
        query_pos = position(t * half + lax.broadcasted_iota(jnp.int32, (half, 1), 0))
        key_pos = position(lax.broadcasted_iota(jnp.int32, (1, rows), 1))
        begin = jnp.zeros((half, 1), jnp.int32)
        end = 0
        for k in range(seq_lens.shape[0]):
            end = end + seq_lens[k]
            begin = jnp.where(query_pos >= end, end, begin)
        visible = (key_pos >= begin) & (key_pos <= query_pos)
        if t == 0:
            kv_swap().wait_recv()
        keys = got_kv[0].reshape(rows, HEAD_SIZE)
        vals = got_kv[1].reshape(rows, HEAD_SIZE)
        for h in range(local_heads):
            cols = slice(h * HEAD_SIZE, (h + 1) * HEAD_SIZE)
            heads = got[t, :, :, :, cols].reshape(half, HEAD_SIZE)
            scores = lax.dot_general(
                heads, keys, (((1,), (1,)), ((), ())), preferred_element_type=F32
            ) * (1.0 / math.sqrt(HEAD_SIZE))
            masked = jnp.where(visible, scores, -1e30)
            highest = jnp.max(masked, axis=1, keepdims=True)
            expo = jnp.where(visible, jnp.exp(masked - highest), 0.0)
            probs = (expo / jnp.sum(expo, axis=1, keepdims=True)).astype(BF16)
            a_ref[t * half : (t + 1) * half, cols] = jnp.dot(
                probs, vals, preferred_element_type=F32
            ).astype(BF16)

    pl.semaphore_wait(barrier, mp - 1)

    @pl.loop(1, mp)
    def _(d):
        kv_copy(d).start()

    @pl.when(core == 0)
    def _():
        send_queries()

    own_q.wait()
    own_kv.wait()

    @pl.loop(1, mp)
    def _(d):
        kv_copy(d).wait_recv()

    kv_swap().start()
    attend(0)

    @pl.when(core == 1)
    def _():
        send_queries()

    square[...] = jnp.zeros_like(square)
    acc[...] = jnp.zeros_like(acc)

    def multiply(u):
        t, j = u // n, lax.rem(u, n)

        @pl.when(t == 0)
        def _():
            w_copy(j, True).wait()

        lhs = a_ref[pl.ds(pl.multiple_of(t * half, half), half), :]
        res = jnp.dot(lhs, w[j, : lhs.shape[1], :], preferred_element_type=F32).astype(BF16)
        part[u, 0] = res[:, :hw]
        part[u, 1] = res[:, hw:]

        @pl.when(t == core)
        def _():
            for c in range(2):
                mine = part[u, c, span(own, tok), :].astype(F32) + res_ref[:, half_columns(j, c)].astype(F32)
                part[u, c, span(own, tok), :] = mine.astype(BF16)

        core_copy(u).start()

        @pl.when(t == 1)
        def _():
            w_copy(j, False).start()

    def add_core(u):
        core_copy(u).wait_recv()
        part[u, core] = (part[u, core].astype(F32) + from_core[u].astype(F32)).astype(BF16)
        one_copy(u).start()

    def add_one(u):
        b1, _, _, _ = order(lax.rem(u, n))
        one_copy(u).wait_recv()
        at = span(b1 * r1, r1)
        part[u, core, at, :] = (part[u, core, at, :].astype(F32) + from_one[u].astype(F32)).astype(BF16)
        two_copy(u).start()

    def add_two(u):
        b1, b2, _, _ = order(lax.rem(u, n))
        two_copy(u).wait_recv()
        at = span(b1 * r1 + b2 * r2, r2)
        part[u, core, at, :] = (part[u, core, at, :].astype(F32) + from_two[u].astype(F32)).astype(BF16)
        z_copy(u, 0).start()

    def add_z(u, k):
        b1, b2, _, _ = order(lax.rem(u, n))
        at = span(b1 * r1 + b2 * r2, r2)
        z_copy(u, k).wait_recv()
        total = (part[u, core, at, :].astype(F32) + from_z[u, k].astype(F32)).astype(BF16)
        if k < bits - 1:
            z_copy(u, k).wait_send()
            part[u, core, at, :] = total
            z_copy(u, k + 1).start()
        else:
            whole[u, core, at, :] = total
            gtwo_copy(u).start()

    def spread_one(u):
        gtwo_copy(u).wait_recv()
        gone_copy(u).start()

    def spread_core(u):
        gone_copy(u).wait_recv()
        gc_copy(u).start()

    def consume(u):
        t, j = u // n, lax.rem(u, n)
        gc_copy(u).wait_recv()

        @pl.when(t == 0)
        def _():
            gate_copy(j).wait()
            up_copy(j).wait()

        @pl.when(t == core)
        def _():
            for c in range(2):
                stream_ref[:, half_columns(j, c)] = whole[u, c, span(own, tok), :]

        total = square[...]
        for c in range(2):
            x = whole[u, c].astype(F32)
            for k in range(0, hw, 128):
                total += x[:, k : k + 128] * x[:, k : k + 128]
            for f in range(gained.shape[0]):
                gained[f, :, c * hw : (c + 1) * hw] = (x * gain_ref[f : f + 1, half_columns(j, c)]).astype(BF16)
        square[...] = total
        for s in range(slices):
            cols = slice(s * SLICE, (s + 1) * SLICE)
            both = jnp.concatenate([gate[j, :, cols], up[j, :, cols]], axis=1)
            acc[s] += jnp.dot(gained[table[me * slices + s]], both, preferred_element_type=F32)

        @pl.when(j == n - 1)
        def _():
            inv = lax.rsqrt(jnp.sum(square[...], axis=1, keepdims=True) / (n * cw) + 1e-05)
            for s in range(slices):
                both = acc[s] * inv
                g, u_ = both[:, :SLICE], both[:, SLICE:]
                hidden[t, :, s * SLICE : (s + 1) * SLICE] = (g / (1.0 + jnp.exp(-g)) * u_).astype(BF16)
            square[...] = jnp.zeros_like(square)
            acc[...] = jnp.zeros_like(acc)

    def multiply_down(u):
        t, j = u // n, lax.rem(u, n)
        core_copy(u).wait_send()
        one_copy(u).wait_send()
        two_copy(u).wait_send()
        z_copy(u, bits - 1).wait_send()

        @pl.when(t == 0)
        def _():
            w_copy(j, False).wait()

        lhs = hidden[t]
        res = jnp.dot(lhs, w[j, : lhs.shape[1], :], preferred_element_type=F32).astype(BF16)
        other = turned(j)
        for a in range(2):
            for b in range(2):
                at = span((a * 2 + b + other * (b - a)) * r2, r2)
                for c in range(2):
                    part[u, c, at, :] = res[(a * 2 + b) * r2 : (a * 2 + b + 1) * r2, c * hw : (c + 1) * hw]

        @pl.when(t != core)
        def _():
            own_core_copy(u).start()

    def mine_only(stage):
        def body(u):
            @pl.when(u // n == core)
            def _():
                stage(u)
        return body

    def own_add_core(u):
        j = lax.rem(u, n)
        own_core_copy(u).wait_recv()
        part[u] = (part[u].astype(F32) + own_core[j].astype(F32)).astype(BF16)
        own_one_copy(u).start()

    def own_add_one(u):
        j = lax.rem(u, n)
        b1, _, _, _ = order(j)
        own_one_copy(u).wait_recv()
        at = span(b1 * r1, r1)
        part[u, :, at, :] = (part[u, :, at, :].astype(F32) + own_one[j].astype(F32)).astype(BF16)
        own_two_copy(u).start()

    def own_add_two(u):
        j = lax.rem(u, n)
        own_two_copy(u).wait_recv()
        at = span(z_start(j, 0), r2)
        part[u, :, at, :] = (part[u, :, at, :].astype(F32) + own_two[j].astype(F32)).astype(BF16)
        own_z_copy(u, 0).start()

    def own_add_z(u, k):
        j = lax.rem(u, n)
        size = r2 >> (k + 1)
        own_z_copy(u, k).wait_recv()
        at = span(z_start(j, k + 1), size)
        total = part[u, :, at, :].astype(F32) + own_z[j, k, :, :size].astype(F32)
        if k < bits - 1:
            part[u, :, at, :] = total.astype(BF16)
            own_z_copy(u, k + 1).start()
        else:
            for c in range(2):
                cols = half_columns(j, c)
                mixed_ref[:, cols] = (stream_ref[:, cols].astype(F32) + total[c]).astype(BF16)

    def run(stages, last):
        @pl.loop(0, last)
        def _(i):
            @pl.when(i == SECOND)
            def _():
                attend(1)

            for lag, stage in stages:
                @pl.when((i >= lag) & (i < 2 * n + lag))
                def _(stage=stage, lag=lag):
                    stage(i - lag)

    first = [(0, multiply)]
    lag = 0
    for gap, stage in zip(GAPS, [add_core, add_one, add_two]):
        lag += gap
        first.append((lag, stage))
    for k in range(bits):
        lag += GAPS[3]
        first.append((lag, functools.partial(add_z, k=k)))
    for gap, stage in zip(GAPS[4:], [spread_one, spread_core, consume]):
        lag += gap
        first.append((lag, stage))
    lag += n
    second = [(lag, multiply_down)]
    for gap, stage in zip(OWN_GAPS, [own_add_core, own_add_one, own_add_two]):
        lag += gap
        second.append((lag, mine_only(stage)))
    for k in range(bits):
        lag += OWN_GAPS[3]
        second.append((lag, mine_only(functools.partial(own_add_z, k=k))))
    run((first + second)[::-1], 2 * n + lag)

    @pl.loop(1, mp)
    def _(d):
        kv_copy(d).wait_send()
        q_copy(d).wait_send()

    kv_swap().wait_send()

    @pl.loop(0, 2 * n)
    def _(u):
        gtwo_copy(u).wait_send()
        gone_copy(u).wait_send()
        gc_copy(u).wait_send()

        @pl.when(u // n != core)
        def _():
            own_core_copy(u).wait_send()

        @pl.when(u // n == core)
        def _():
            own_one_copy(u).wait_send()
            own_two_copy(u).wait_send()
            for k in range(bits):
                own_z_copy(u, k).wait_send()


def layer(seq_lens, table, queries, keys, vals, tokens, gain, out_weight, gate_weight, up_weight,
          down_weight, zs):
    tok, width = tokens.shape
    depth = out_weight.shape[0]
    mp = 4 * zs
    rows = tok * mp
    assert tok & (tok - 1) == 0 and zs & (zs - 1) == 0 and zs >= 4
    units = down_weight.shape[0]
    slices = units // SLICE
    n, cw, half = CHUNKS, width // CHUNKS, rows // 2
    hw = cw // 2
    bits = zs.bit_length() - 2
    dma = pltpu.SemaphoreType.DMA
    vmem = pl.BlockSpec(memory_space=pltpu.VMEM)
    hbm = pl.BlockSpec(memory_space=pl.ANY)
    m = 2 * n
    return pl.pallas_call(
        functools.partial(layer_kernel, zs, slices),
        out_shape=jax.ShapeDtypeStruct((2, tok, width), BF16),
        in_specs=[pl.BlockSpec(memory_space=pltpu.SMEM)] * 2 + [vmem] * 5 + [hbm] * 4,
        out_specs=vmem,
        scratch_shapes=[
            pltpu.VMEM((mp, tok, HEAD_SIZE), BF16),
            pltpu.VMEM((2, 2, zs, tok, depth), BF16),
            pltpu.VMEM((2, 2, 2, zs, tok, HEAD_SIZE), BF16),
            pltpu.VMEM((rows, depth), BF16),
            dma((mp,)), dma((mp,)), dma((mp,)), dma((mp,)), dma((1,)), dma((1,)), dma((2,)),
            pltpu.VMEM((n, max(depth, units), cw), BF16),
            pltpu.VMEM((n, cw, units), BF16),
            pltpu.VMEM((n, cw, units), BF16),
            pltpu.VMEM((m, 2, half, hw), BF16),
            pltpu.VMEM((m, 2, half, hw), BF16),
            pltpu.VMEM((m, half, hw), BF16),
            pltpu.VMEM((m, half // 2, hw), BF16),
            pltpu.VMEM((m, half // 4, hw), BF16),
            pltpu.VMEM((m, bits, half // 4, hw), BF16),
            pltpu.VMEM((n, 2, half, hw), BF16),
            pltpu.VMEM((n, 2, half // 2, hw), BF16),
            pltpu.VMEM((n, 2, half // 4, hw), BF16),
            pltpu.VMEM((n, bits, 2, half // 8, hw), BF16),
            pltpu.VMEM((gain.shape[0], half, cw), BF16),
            pltpu.VMEM((half, 128), F32),
            pltpu.VMEM((slices, half, 2 * SLICE), F32),
            pltpu.VMEM((2, half, units), BF16),
            dma((n,)), dma((n,)), dma((n,)),
            dma((m,)), dma((m,)), dma((m,)), dma((m,)), dma((m,)), dma((m,)), dma((m, bits)), dma((m, bits)),
            dma((m,)), dma((m,)), dma((m,)), dma((m,)), dma((m,)), dma((m,)),
            dma((n,)), dma((n,)), dma((n,)), dma((n,)), dma((n,)), dma((n,)), dma((n, bits)), dma((n, bits)),
        ],
        compiler_params=pltpu.CompilerParams(
            collective_id=0, has_side_effects=True, vmem_limit_bytes=62 << 20
        ),
        name="layer",
    )(seq_lens, table, queries, keys, vals, tokens, gain, out_weight, gate_weight, up_weight, down_weight)


def local(tokens, queries, key_proj, values, seq_lens, out_weight, ffn_gain, gate_weight, up_weight,
          down_weight, slice_table):
    both = layer(
        seq_lens, slice_table, queries, key_proj, values, tokens, ffn_gain, out_weight, gate_weight,
        up_weight, down_weight, lax.axis_size("mp") // 4
    )
    stream, mixed = both[0], both[1]
    return (stream, mixed)


def solution(mesh):
    placed = (
        P(("groups", "mp"), None),
        P(("groups", "mp"), None),
        P(("groups", "mp"), None),
        P(("groups", "mp"), None),
        P("groups"),
        P("mp", None),
        P(),
        P(None, "mp"),
        P(None, "mp"),
        P("mp", None),
        P(),
    )
    return jax.shard_map(
        local,
        mesh=mesh,
        in_specs=placed,
        out_specs=(P(("groups", "mp"), None), P(("groups", "mp"), None)),
        check_vma=False,
    )
```

```python
import functools
import math

import jax
import jax.numpy as jnp
from jax import lax
from jax.experimental import pallas as pl
from jax.experimental.pallas import tpu as pltpu
from jax.sharding import PartitionSpec as P

QUERY_HEADS = 64
HEAD_SIZE = 128
SLICE = 128
CHUNKS = 8
TURN = 8
OWN_TURN = 4
GAPS = (2, 4, 3, 3, 3, 4, 2)
OWN_GAPS = (1, 4, 4, 4)
SECOND = 8
MESH = pl.DeviceIdType.MESH
F32 = jnp.float32
BF16 = jnp.bfloat16


def flip(z, zs):
    bits = zs.bit_length() - 1
    out = 0
    for k in range(bits):
        out = out + ((z >> k) & 1) * (1 << (bits - 1 - k))
    return out


def layer_kernel(zs, slices, *refs):
    (seq_lens, table, q_ref, k_ref, v_ref, res_ref, gain_ref, w_hbm, gate_hbm, up_hbm, down_hbm,
     both_ref, packed, got, got_kv, a_ref, ps, pr, ks, kr, ws, wr, self_sem, w, gate, up, part, whole, from_core, from_one, from_two, from_z,
     own_core, own_one, own_two, own_z, gained, square, acc, hidden,
     w_sem, gate_sem, up_sem, cs, cr, os, orr, ts, tr, zsend, zrecv, gts, gtr, gos, gor, gcs, gcr,
     rcs, rcr, ros, ror, rts, rtr, rzs, rzr) = refs
    n = w.shape[0]
    half, hw = part.shape[2], part.shape[3]
    rows, cw = 2 * half, 2 * hw
    tok = res_ref.shape[0]
    mp = 4 * zs
    r1, r2 = half // 2, half // 4
    bits = from_z.shape[1]
    q_width = got.shape[4]
    me = lax.axis_index("mp")
    core, y, z = lax.rem(me, 2), lax.rem(me // 2, 2), me // 4
    zr = flip(z, zs)
    near = lax.rem(z, 2)
    own = (y * zs + zr) * tok
    stream_ref, mixed_ref = both_ref.at[0], both_ref.at[1]

    def dev(z_, y_, core_):
        return {"mp": (z_ * 2 + y_) * 2 + core_}

    across_core = dev(z, y, 1 - core)

    def turned(j, every=OWN_TURN):
        return jnp.int32(lax.rem(j, every) == every - 2)

    def order(j, every=OWN_TURN):
        t = turned(j, every)
        b1 = y + t * (near - y)
        b2 = near + t * (y - near)
        flip_y = z * 2 + 1 - y
        flip_z = (z + 1 - 2 * near) * 2 + y
        one = flip_y + t * (flip_z - flip_y)
        two = flip_z + t * (flip_y - flip_z)
        return b1, b2, {"mp": one * 2 + core}, {"mp": two * 2 + core}

    def z_partner(k):
        bit = 2 << k
        up_bit = (z // bit) & 1
        return dev(z + bit * (1 - 2 * up_bit), y, core), up_bit

    def columns(j):
        return pl.ds(pl.multiple_of(j * cw, cw), cw)

    def half_columns(j, c):
        return pl.ds(pl.multiple_of(j * cw + c * hw, hw), hw)

    def span(start, size):
        return pl.ds(pl.multiple_of(start, tok), size)

    def w_copy(j, first):
        src = w_hbm if first else down_hbm
        dst = w.at[j, pl.ds(0, src.shape[0])]
        return pltpu.make_async_copy(src.at[:, columns(j)], dst, w_sem.at[j])

    def gate_copy(j):
        return pltpu.make_async_copy(gate_hbm.at[columns(j), :], gate.at[j], gate_sem.at[j])

    def up_copy(j):
        return pltpu.make_async_copy(up_hbm.at[columns(j), :], up.at[j], up_sem.at[j])

    def remote(src, dst, s, r, to):
        return pltpu.make_async_remote_copy(
            src_ref=src, dst_ref=dst, send_sem=s, recv_sem=r, device_id=to, device_id_type=MESH
        )

    def core_copy(u):
        return remote(part.at[u, 1 - core], from_core.at[u], cs.at[u], cr.at[u], across_core)

    def one_copy(u):
        b1, _, to, _ = order(lax.rem(u, n), TURN)
        return remote(part.at[u, core, span((1 - b1) * r1, r1)], from_one.at[u], os.at[u], orr.at[u], to)

    def two_copy(u):
        b1, b2, _, to = order(lax.rem(u, n), TURN)
        src = part.at[u, core, span(b1 * r1 + (1 - b2) * r2, r2)]
        return remote(src, from_two.at[u], ts.at[u], tr.at[u], to)

    def z_copy(u, k):
        b1, b2, _, _ = order(lax.rem(u, n), TURN)
        src = part.at[u, core, span(b1 * r1 + b2 * r2, r2)]
        return remote(src, from_z.at[u, k], zsend.at[u, k], zrecv.at[u, k], z_partner(k)[0])

    def gtwo_copy(u):
        b1, b2, _, to = order(lax.rem(u, n), TURN)
        mine = whole.at[u, core, span(b1 * r1 + b2 * r2, r2)]
        return remote(mine, mine, gts.at[u], gtr.at[u], to)

    def gone_copy(u):
        b1, _, to, _ = order(lax.rem(u, n), TURN)
        mine = whole.at[u, core, span(b1 * r1, r1)]
        return remote(mine, mine, gos.at[u], gor.at[u], to)

    def gc_copy(u):
        mine = whole.at[u, core]
        return remote(mine, mine, gcs.at[u], gcr.at[u], across_core)

    def own_core_copy(u):
        j = lax.rem(u, n)
        return remote(part.at[u], own_core.at[j], rcs.at[j], rcr.at[j], across_core)

    def own_one_copy(u):
        j = lax.rem(u, n)
        b1, _, to, _ = order(j)
        src = part.at[u, :, span((1 - b1) * r1, r1)]
        return remote(src, own_one.at[j], ros.at[j], ror.at[j], to)

    def own_two_copy(u):
        j = lax.rem(u, n)
        b1, b2, _, to = order(j)
        src = part.at[u, :, span(b1 * r1 + (1 - b2) * r2, r2)]
        return remote(src, own_two.at[j], rts.at[j], rtr.at[j], to)

    def z_start(j, k):
        b1, b2, _, _ = order(j)
        start = b1 * r1 + b2 * r2
        for i in range(k):
            start = start + z_partner(i)[1] * (r2 >> (i + 1))
        return start

    def own_z_copy(u, k):
        j = lax.rem(u, n)
        to, up_bit = z_partner(k)
        size = r2 >> (k + 1)
        src = part.at[u, :, span(z_start(j, k) + (1 - up_bit) * size, size)]
        return remote(src, own_z.at[j, k, :, pl.ds(0, size)], rzs.at[j, k], rzr.at[j, k], to)

    def q_columns(to):
        return pl.ds(pl.multiple_of(to * q_width, q_width), q_width)

    def q_copy(d):
        to = lax.rem(me + d, mp)
        return remote(q_ref.at[:, q_columns(to)], got.at[core, y, zr], ps.at[d], pr.at[d], {"mp": to})

    def kv_copy(d):
        to = lax.rem(me + d, mp)
        return remote(packed.at[to], got_kv.at[lax.rem(to, 2), core, y, zr], ks.at[d], kr.at[d], {"mp": to})

    def kv_swap():
        mine = got_kv.at[core]
        return remote(mine, mine, ws.at[0], wr.at[0], across_core)

    own_q = pltpu.make_async_copy(q_ref.at[:, q_columns(me)], got.at[core, y, zr], self_sem.at[0])
    own_kv = pltpu.make_async_copy(packed.at[me], got_kv.at[core, core, y, zr], self_sem.at[1])

    barrier = pltpu.get_barrier_semaphore()

    @pl.loop(1, mp)
    def _(d):
        pl.semaphore_signal(
            barrier, inc=1, device_id={"mp": lax.rem(me + d, mp)}, device_id_type=MESH
        )

    @pl.loop(0, n)
    def _(j):
        w_copy(j, True).start()

    @pl.loop(0, n)
    def _(j):
        gate_copy(j).start()
        up_copy(j).start()

    heads_kv = k_ref.shape[1] // HEAD_SIZE
    per_group = QUERY_HEADS // heads_kv
    local_heads = q_width // HEAD_SIZE
    assert per_group % (2 * local_heads) == 0
    for to in range(mp):
        head = to * local_heads // per_group
        cols = slice(head * HEAD_SIZE, (head + 1) * HEAD_SIZE)
        packed[to] = (v_ref if to % 2 else k_ref)[:, cols]
    own_q.start()
    own_kv.start()

    def position(at):
        token, block = at & (tok - 1), at // tok
        z_at = flip(block & (zs - 1), zs)
        y_at, core_at = (block // zs) & 1, block // (zs * 2)
        return ((z_at * 2 + y_at) * 2 + core_at) * tok + token

    def send_queries():
        @pl.loop(1, mp)
        def _(d):
            q_copy(d).start()

    def from_half(t, act):
        @pl.loop(1, mp)
        def _(d):
            @pl.when(lax.rem(me + d, 2) == t)
            def _():
                act(d)

    def attend(t):
        from_half(t, lambda d: q_copy(d).wait_recv())
        query_pos = position(t * half + lax.broadcasted_iota(jnp.int32, (half, 1), 0))
        key_pos = position(lax.broadcasted_iota(jnp.int32, (1, rows), 1))
        begin = jnp.zeros((half, 1), jnp.int32)
        end = 0
        for k in range(seq_lens.shape[0]):
            end = end + seq_lens[k]
            begin = jnp.where(query_pos >= end, end, begin)
        visible = (key_pos >= begin) & (key_pos <= query_pos)
        if t == 0:
            kv_swap().wait_recv()
        keys = got_kv[0].reshape(rows, HEAD_SIZE)
        vals = got_kv[1].reshape(rows, HEAD_SIZE)
        for h in range(local_heads):
            cols = slice(h * HEAD_SIZE, (h + 1) * HEAD_SIZE)
            heads = got[t, :, :, :, cols].reshape(half, HEAD_SIZE)
            scores = lax.dot_general(
                heads, keys, (((1,), (1,)), ((), ())), preferred_element_type=F32
            ) * (1.0 / math.sqrt(HEAD_SIZE))
            masked = jnp.where(visible, scores, -1e30)
            highest = jnp.max(masked, axis=1, keepdims=True)
            expo = jnp.where(visible, jnp.exp(masked - highest), 0.0)
            probs = (expo / jnp.sum(expo, axis=1, keepdims=True)).astype(BF16)
            a_ref[t * half : (t + 1) * half, cols] = jnp.dot(
                probs, vals, preferred_element_type=F32
            ).astype(BF16)

    pl.semaphore_wait(barrier, mp - 1)

    @pl.loop(1, mp)
    def _(d):
        kv_copy(d).start()

    @pl.when(core == 0)
    def _():
        send_queries()

    own_q.wait()
    own_kv.wait()

    @pl.loop(1, mp)
    def _(d):
        kv_copy(d).wait_recv()

    kv_swap().start()
    attend(0)

    @pl.when(core == 1)
    def _():
        send_queries()

    square[...] = jnp.zeros_like(square)
    acc[...] = jnp.zeros_like(acc)

    def multiply(u):
        t, j = u // n, lax.rem(u, n)

        @pl.when(t == 0)
        def _():
            w_copy(j, True).wait()

        lhs = a_ref[pl.ds(pl.multiple_of(t * half, half), half), :]
        res = jnp.dot(lhs, w[j, : lhs.shape[1], :], preferred_element_type=F32).astype(BF16)
        part[u, 0] = res[:, :hw]
        part[u, 1] = res[:, hw:]

        @pl.when(t == core)
        def _():
            for c in range(2):
                mine = part[u, c, span(own, tok), :].astype(F32) + res_ref[:, half_columns(j, c)].astype(F32)
                part[u, c, span(own, tok), :] = mine.astype(BF16)

        core_copy(u).start()

        @pl.when(t == 1)
        def _():
            w_copy(j, False).start()

    def add_core(u):
        core_copy(u).wait_recv()
        part[u, core] = (part[u, core].astype(F32) + from_core[u].astype(F32)).astype(BF16)
        one_copy(u).start()

    def add_one(u):
        b1, _, _, _ = order(lax.rem(u, n), TURN)
        one_copy(u).wait_recv()
        at = span(b1 * r1, r1)
        part[u, core, at, :] = (part[u, core, at, :].astype(F32) + from_one[u].astype(F32)).astype(BF16)
        two_copy(u).start()

    def add_two(u):
        b1, b2, _, _ = order(lax.rem(u, n), TURN)
        two_copy(u).wait_recv()
        at = span(b1 * r1 + b2 * r2, r2)
        part[u, core, at, :] = (part[u, core, at, :].astype(F32) + from_two[u].astype(F32)).astype(BF16)
        z_copy(u, 0).start()

    def add_z(u, k):
        b1, b2, _, _ = order(lax.rem(u, n), TURN)
        at = span(b1 * r1 + b2 * r2, r2)
        z_copy(u, k).wait_recv()
        total = (part[u, core, at, :].astype(F32) + from_z[u, k].astype(F32)).astype(BF16)
        if k < bits - 1:
            z_copy(u, k).wait_send()
            part[u, core, at, :] = total
            z_copy(u, k + 1).start()
        else:
            whole[u, core, at, :] = total
            gtwo_copy(u).start()

    def spread_one(u):
        gtwo_copy(u).wait_recv()
        gone_copy(u).start()

    def spread_core(u):
        gone_copy(u).wait_recv()
        gc_copy(u).start()

    def consume(u):
        t, j = u // n, lax.rem(u, n)
        gc_copy(u).wait_recv()

        @pl.when(t == 0)
        def _():
            gate_copy(j).wait()
            up_copy(j).wait()

        @pl.when(t == core)
        def _():
            for c in range(2):
                stream_ref[:, half_columns(j, c)] = whole[u, c, span(own, tok), :]

        total = square[...]
        for c in range(2):
            x = whole[u, c].astype(F32)
            for k in range(0, hw, 128):
                total += x[:, k : k + 128] * x[:, k : k + 128]
            for f in range(gained.shape[0]):
                gained[f, :, c * hw : (c + 1) * hw] = (x * gain_ref[f : f + 1, half_columns(j, c)]).astype(BF16)
        square[...] = total
        for s in range(slices):
            cols = slice(s * SLICE, (s + 1) * SLICE)
            both = jnp.concatenate([gate[j, :, cols], up[j, :, cols]], axis=1)
            acc[s] += jnp.dot(gained[table[me * slices + s]], both, preferred_element_type=F32)

        @pl.when(j == n - 1)
        def _():
            inv = lax.rsqrt(jnp.sum(square[...], axis=1, keepdims=True) / (n * cw) + 1e-05)
            for s in range(slices):
                both = acc[s] * inv
                g, u_ = both[:, :SLICE], both[:, SLICE:]
                hidden[t, :, s * SLICE : (s + 1) * SLICE] = (g / (1.0 + jnp.exp(-g)) * u_).astype(BF16)
            square[...] = jnp.zeros_like(square)
            acc[...] = jnp.zeros_like(acc)

    def multiply_down(u):
        t, j = u // n, lax.rem(u, n)
        core_copy(u).wait_send()
        one_copy(u).wait_send()
        two_copy(u).wait_send()
        z_copy(u, bits - 1).wait_send()

        @pl.when(t == 0)
        def _():
            w_copy(j, False).wait()

        lhs = hidden[t]
        res = jnp.dot(lhs, w[j, : lhs.shape[1], :], preferred_element_type=F32).astype(BF16)
        other = turned(j)
        for a in range(2):
            for b in range(2):
                at = span((a * 2 + b + other * (b - a)) * r2, r2)
                for c in range(2):
                    part[u, c, at, :] = res[(a * 2 + b) * r2 : (a * 2 + b + 1) * r2, c * hw : (c + 1) * hw]

        @pl.when(t != core)
        def _():
            own_core_copy(u).start()

    def mine_only(stage):
        def body(u):
            @pl.when(u // n == core)
            def _():
                stage(u)
        return body

    def own_add_core(u):
        j = lax.rem(u, n)
        own_core_copy(u).wait_recv()
        part[u] = (part[u].astype(F32) + own_core[j].astype(F32)).astype(BF16)
        own_one_copy(u).start()

    def own_add_one(u):
        j = lax.rem(u, n)
        b1, _, _, _ = order(j)
        own_one_copy(u).wait_recv()
        at = span(b1 * r1, r1)
        part[u, :, at, :] = (part[u, :, at, :].astype(F32) + own_one[j].astype(F32)).astype(BF16)
        own_two_copy(u).start()

    def own_add_two(u):
        j = lax.rem(u, n)
        own_two_copy(u).wait_recv()
        at = span(z_start(j, 0), r2)
        part[u, :, at, :] = (part[u, :, at, :].astype(F32) + own_two[j].astype(F32)).astype(BF16)
        own_z_copy(u, 0).start()

    def own_add_z(u, k):
        j = lax.rem(u, n)
        size = r2 >> (k + 1)
        own_z_copy(u, k).wait_recv()
        at = span(z_start(j, k + 1), size)
        total = part[u, :, at, :].astype(F32) + own_z[j, k, :, :size].astype(F32)
        if k < bits - 1:
            part[u, :, at, :] = total.astype(BF16)
            own_z_copy(u, k + 1).start()
        else:
            for c in range(2):
                cols = half_columns(j, c)
                mixed_ref[:, cols] = (stream_ref[:, cols].astype(F32) + total[c]).astype(BF16)

    def run(stages, last):
        @pl.loop(0, last)
        def _(i):
            @pl.when(i == SECOND)
            def _():
                attend(1)

            for lag, stage in stages:
                @pl.when((i >= lag) & (i < 2 * n + lag))
                def _(stage=stage, lag=lag):
                    stage(i - lag)

    first = [(0, multiply)]
    lag = 0
    for gap, stage in zip(GAPS, [add_core, add_one, add_two]):
        lag += gap
        first.append((lag, stage))
    for k in range(bits):
        lag += GAPS[3]
        first.append((lag, functools.partial(add_z, k=k)))
    for gap, stage in zip(GAPS[4:], [spread_one, spread_core, consume]):
        lag += gap
        first.append((lag, stage))
    lag += n
    second = [(lag, multiply_down)]
    for gap, stage in zip(OWN_GAPS, [own_add_core, own_add_one, own_add_two]):
        lag += gap
        second.append((lag, mine_only(stage)))
    for k in range(bits):
        lag += OWN_GAPS[3]
        second.append((lag, mine_only(functools.partial(own_add_z, k=k))))
    run((first + second)[::-1], 2 * n + lag)

    @pl.loop(1, mp)
    def _(d):
        kv_copy(d).wait_send()
        q_copy(d).wait_send()

    kv_swap().wait_send()

    @pl.loop(0, 2 * n)
    def _(u):
        gtwo_copy(u).wait_send()
        gone_copy(u).wait_send()
        gc_copy(u).wait_send()

        @pl.when(u // n != core)
        def _():
            own_core_copy(u).wait_send()

        @pl.when(u // n == core)
        def _():
            own_one_copy(u).wait_send()
            own_two_copy(u).wait_send()
            for k in range(bits):
                own_z_copy(u, k).wait_send()


def layer(seq_lens, table, queries, keys, vals, tokens, gain, out_weight, gate_weight, up_weight,
          down_weight, zs):
    tok, width = tokens.shape
    depth = out_weight.shape[0]
    mp = 4 * zs
    rows = tok * mp
    assert tok & (tok - 1) == 0 and zs & (zs - 1) == 0 and zs >= 4
    units = down_weight.shape[0]
    slices = units // SLICE
    n, cw, half = CHUNKS, width // CHUNKS, rows // 2
    hw = cw // 2
    bits = zs.bit_length() - 2
    dma = pltpu.SemaphoreType.DMA
    vmem = pl.BlockSpec(memory_space=pltpu.VMEM)
    hbm = pl.BlockSpec(memory_space=pl.ANY)
    m = 2 * n
    return pl.pallas_call(
        functools.partial(layer_kernel, zs, slices),
        out_shape=jax.ShapeDtypeStruct((2, tok, width), BF16),
        in_specs=[pl.BlockSpec(memory_space=pltpu.SMEM)] * 2 + [vmem] * 5 + [hbm] * 4,
        out_specs=vmem,
        scratch_shapes=[
            pltpu.VMEM((mp, tok, HEAD_SIZE), BF16),
            pltpu.VMEM((2, 2, zs, tok, depth), BF16),
            pltpu.VMEM((2, 2, 2, zs, tok, HEAD_SIZE), BF16),
            pltpu.VMEM((rows, depth), BF16),
            dma((mp,)), dma((mp,)), dma((mp,)), dma((mp,)), dma((1,)), dma((1,)), dma((2,)),
            pltpu.VMEM((n, max(depth, units), cw), BF16),
            pltpu.VMEM((n, cw, units), BF16),
            pltpu.VMEM((n, cw, units), BF16),
            pltpu.VMEM((m, 2, half, hw), BF16),
            pltpu.VMEM((m, 2, half, hw), BF16),
            pltpu.VMEM((m, half, hw), BF16),
            pltpu.VMEM((m, half // 2, hw), BF16),
            pltpu.VMEM((m, half // 4, hw), BF16),
            pltpu.VMEM((m, bits, half // 4, hw), BF16),
            pltpu.VMEM((n, 2, half, hw), BF16),
            pltpu.VMEM((n, 2, half // 2, hw), BF16),
            pltpu.VMEM((n, 2, half // 4, hw), BF16),
            pltpu.VMEM((n, bits, 2, half // 8, hw), BF16),
            pltpu.VMEM((gain.shape[0], half, cw), BF16),
            pltpu.VMEM((half, 128), F32),
            pltpu.VMEM((slices, half, 2 * SLICE), F32),
            pltpu.VMEM((2, half, units), BF16),
            dma((n,)), dma((n,)), dma((n,)),
            dma((m,)), dma((m,)), dma((m,)), dma((m,)), dma((m,)), dma((m,)), dma((m, bits)), dma((m, bits)),
            dma((m,)), dma((m,)), dma((m,)), dma((m,)), dma((m,)), dma((m,)),
            dma((n,)), dma((n,)), dma((n,)), dma((n,)), dma((n,)), dma((n,)), dma((n, bits)), dma((n, bits)),
        ],
        compiler_params=pltpu.CompilerParams(
            collective_id=0, has_side_effects=True, vmem_limit_bytes=62 << 20
        ),
        name="layer",
    )(seq_lens, table, queries, keys, vals, tokens, gain, out_weight, gate_weight, up_weight, down_weight)


def local(tokens, queries, key_proj, values, seq_lens, out_weight, ffn_gain, gate_weight, up_weight,
          down_weight, slice_table):
    both = layer(
        seq_lens, slice_table, queries, key_proj, values, tokens, ffn_gain, out_weight, gate_weight,
        up_weight, down_weight, lax.axis_size("mp") // 4
    )
    stream, mixed = both[0], both[1]
    return (stream, mixed)


def solution(mesh):
    placed = (
        P(("groups", "mp"), None),
        P(("groups", "mp"), None),
        P(("groups", "mp"), None),
        P(("groups", "mp"), None),
        P("groups"),
        P("mp", None),
        P(),
        P(None, "mp"),
        P(None, "mp"),
        P("mp", None),
        P(),
    )
    return jax.shard_map(
        local,
        mesh=mesh,
        in_specs=placed,
        out_specs=(P(("groups", "mp"), None), P(("groups", "mp"), None)),
        check_vma=False,
    )
```

```python
import functools
import math

import jax
import jax.numpy as jnp
from jax import lax
from jax.experimental import pallas as pl
from jax.experimental.pallas import tpu as pltpu
from jax.sharding import PartitionSpec as P

QUERY_HEADS = 64
HEAD_SIZE = 128
SLICE = 128
CHUNKS = 8
TURN = 8
OWN_TURN = 4
GAPS = (2, 4, 3, 3, 3, 4, 2)
OWN_GAPS = (1, 4, 4, 4)
SECOND = 8
MESH = pl.DeviceIdType.MESH
F32 = jnp.float32
BF16 = jnp.bfloat16


def flip(z, zs):
    bits = zs.bit_length() - 1
    out = 0
    for k in range(bits):
        out = out + ((z >> k) & 1) * (1 << (bits - 1 - k))
    return out


def layer_kernel(zs, slices, *refs):
    (seq_lens, table, q_ref, k_ref, v_ref, res_ref, gain_ref, w_hbm, gate_hbm, up_hbm, down_hbm,
     both_ref, packed, got, got_kv, a_ref, ps, pr, ks, kr, ws, wr, self_sem, w, gate, up, part, whole, from_core, from_one, from_two, from_z,
     own_core, own_one, own_two, own_z, gained, square, acc, hidden,
     w_sem, gate_sem, up_sem, cs, cr, os, orr, ts, tr, zsend, zrecv, gts, gtr, gos, gor, gcs, gcr,
     rcs, rcr, ros, ror, rts, rtr, rzs, rzr) = refs
    n = w.shape[0]
    half, hw = part.shape[2], part.shape[3]
    rows, cw = 2 * half, 2 * hw
    tok = res_ref.shape[0]
    mp = 4 * zs
    r1, r2 = half // 2, half // 4
    bits = from_z.shape[1]
    q_width = got.shape[4]
    me = lax.axis_index("mp")
    core, y, z = lax.rem(me, 2), lax.rem(me // 2, 2), me // 4
    zr = flip(z, zs)
    near = lax.rem(z, 2)
    own = (y * zs + zr) * tok
    stream_ref, mixed_ref = both_ref.at[0], both_ref.at[1]

    def dev(z_, y_, core_):
        return {"mp": (z_ * 2 + y_) * 2 + core_}

    across_core = dev(z, y, 1 - core)

    def turned(j, every=OWN_TURN):
        return jnp.int32(lax.rem(j, every) == every - 2)

    def order(j, every=OWN_TURN):
        t = turned(j, every)
        b1 = y + t * (near - y)
        b2 = near + t * (y - near)
        flip_y = z * 2 + 1 - y
        flip_z = (z + 1 - 2 * near) * 2 + y
        one = flip_y + t * (flip_z - flip_y)
        two = flip_z + t * (flip_y - flip_z)
        return b1, b2, {"mp": one * 2 + core}, {"mp": two * 2 + core}

    def z_partner(k):
        bit = 2 << k
        up_bit = (z // bit) & 1
        return dev(z + bit * (1 - 2 * up_bit), y, core), up_bit

    def columns(j):
        return pl.ds(pl.multiple_of(j * cw, cw), cw)

    def half_columns(j, c):
        return pl.ds(pl.multiple_of(j * cw + c * hw, hw), hw)

    def span(start, size):
        return pl.ds(pl.multiple_of(start, tok), size)

    def w_copy(j, first):
        src = w_hbm if first else down_hbm
        dst = w.at[j, pl.ds(0, src.shape[0])]
        return pltpu.make_async_copy(src.at[:, columns(j)], dst, w_sem.at[j])

    def gate_copy(j):
        return pltpu.make_async_copy(gate_hbm.at[columns(j), :], gate.at[j], gate_sem.at[j])

    def up_copy(j):
        return pltpu.make_async_copy(up_hbm.at[columns(j), :], up.at[j], up_sem.at[j])

    def remote(src, dst, s, r, to):
        return pltpu.make_async_remote_copy(
            src_ref=src, dst_ref=dst, send_sem=s, recv_sem=r, device_id=to, device_id_type=MESH
        )

    def core_copy(u):
        return remote(part.at[u, 1 - core], from_core.at[u], cs.at[u], cr.at[u], across_core)

    def one_copy(u):
        b1, _, to, _ = order(lax.rem(u, n), TURN)
        return remote(part.at[u, core, span((1 - b1) * r1, r1)], from_one.at[u], os.at[u], orr.at[u], to)

    def two_copy(u):
        b1, b2, _, to = order(lax.rem(u, n), TURN)
        src = part.at[u, core, span(b1 * r1 + (1 - b2) * r2, r2)]
        return remote(src, from_two.at[u], ts.at[u], tr.at[u], to)

    def z_copy(u, k):
        b1, b2, _, _ = order(lax.rem(u, n), TURN)
        src = part.at[u, core, span(b1 * r1 + b2 * r2, r2)]
        return remote(src, from_z.at[u, k], zsend.at[u, k], zrecv.at[u, k], z_partner(k)[0])

    def gtwo_copy(u):
        b1, b2, _, to = order(lax.rem(u, n), TURN)
        mine = whole.at[u, core, span(b1 * r1 + b2 * r2, r2)]
        return remote(mine, mine, gts.at[u], gtr.at[u], to)

    def gone_copy(u):
        b1, _, to, _ = order(lax.rem(u, n), TURN)
        mine = whole.at[u, core, span(b1 * r1, r1)]
        return remote(mine, mine, gos.at[u], gor.at[u], to)

    def gc_copy(u):
        mine = whole.at[u, core]
        return remote(mine, mine, gcs.at[u], gcr.at[u], across_core)

    def own_core_copy(u):
        j = lax.rem(u, n)
        return remote(part.at[u], own_core.at[j], rcs.at[j], rcr.at[j], across_core)

    def own_one_copy(u):
        j = lax.rem(u, n)
        b1, _, to, _ = order(j)
        src = part.at[u, :, span((1 - b1) * r1, r1)]
        return remote(src, own_one.at[j], ros.at[j], ror.at[j], to)

    def own_two_copy(u):
        j = lax.rem(u, n)
        b1, b2, _, to = order(j)
        src = part.at[u, :, span(b1 * r1 + (1 - b2) * r2, r2)]
        return remote(src, own_two.at[j], rts.at[j], rtr.at[j], to)

    def z_start(j, k):
        b1, b2, _, _ = order(j)
        start = b1 * r1 + b2 * r2
        for i in range(k):
            start = start + z_partner(i)[1] * (r2 >> (i + 1))
        return start

    def own_z_copy(u, k):
        j = lax.rem(u, n)
        to, up_bit = z_partner(k)
        size = r2 >> (k + 1)
        src = part.at[u, :, span(z_start(j, k) + (1 - up_bit) * size, size)]
        return remote(src, own_z.at[j, k, :, pl.ds(0, size)], rzs.at[j, k], rzr.at[j, k], to)

    def q_columns(to):
        return pl.ds(pl.multiple_of(to * q_width, q_width), q_width)

    def q_copy(d):
        to = lax.rem(me + d, mp)
        return remote(q_ref.at[:, q_columns(to)], got.at[core, y, zr], ps.at[d], pr.at[d], {"mp": to})

    def kv_copy(d):
        to = lax.rem(me + d, mp)
        return remote(packed.at[to], got_kv.at[lax.rem(to, 2), core, y, zr], ks.at[d], kr.at[d], {"mp": to})

    def kv_swap():
        mine = got_kv.at[core]
        return remote(mine, mine, ws.at[0], wr.at[0], across_core)

    own_q = pltpu.make_async_copy(q_ref.at[:, q_columns(me)], got.at[core, y, zr], self_sem.at[0])
    own_kv = pltpu.make_async_copy(packed.at[me], got_kv.at[core, core, y, zr], self_sem.at[1])

    barrier = pltpu.get_barrier_semaphore()

    @pl.loop(1, mp)
    def _(d):
        pl.semaphore_signal(
            barrier, inc=1, device_id={"mp": lax.rem(me + d, mp)}, device_id_type=MESH
        )

    @pl.loop(0, n)
    def _(j):
        w_copy(j, True).start()

    @pl.loop(0, n)
    def _(j):
        gate_copy(j).start()
        up_copy(j).start()

    heads_kv = k_ref.shape[1] // HEAD_SIZE
    per_group = QUERY_HEADS // heads_kv
    local_heads = q_width // HEAD_SIZE
    assert per_group % (2 * local_heads) == 0
    for to in range(mp):
        head = to * local_heads // per_group
        cols = slice(head * HEAD_SIZE, (head + 1) * HEAD_SIZE)
        packed[to] = (v_ref if to % 2 else k_ref)[:, cols]
    own_q.start()
    own_kv.start()

    def position(at):
        token, block = at & (tok - 1), at // tok
        z_at = flip(block & (zs - 1), zs)
        y_at, core_at = (block // zs) & 1, block // (zs * 2)
        return ((z_at * 2 + y_at) * 2 + core_at) * tok + token

    def send_queries():
        @pl.loop(1, mp)
        def _(d):
            q_copy(d).start()

    def from_half(t, act):
        @pl.loop(1, mp)
        def _(d):
            @pl.when(lax.rem(me + d, 2) == t)
            def _():
                act(d)

    def attend(t):
        from_half(t, lambda d: q_copy(d).wait_recv())
        if t == 0:
            @pl.when(core == 1)
            def _():
                send_queries()

        query_pos = position(t * half + lax.broadcasted_iota(jnp.int32, (half, 1), 0))
        key_pos = position(lax.broadcasted_iota(jnp.int32, (1, rows), 1))
        begin = jnp.zeros((half, 1), jnp.int32)
        end = 0
        for k in range(seq_lens.shape[0]):
            end = end + seq_lens[k]
            begin = jnp.where(query_pos >= end, end, begin)
        visible = (key_pos >= begin) & (key_pos <= query_pos)
        if t == 0:
            kv_swap().wait_recv()
        keys = got_kv[0].reshape(rows, HEAD_SIZE)
        vals = got_kv[1].reshape(rows, HEAD_SIZE)
        for h in range(local_heads):
            cols = slice(h * HEAD_SIZE, (h + 1) * HEAD_SIZE)
            heads = got[t, :, :, :, cols].reshape(half, HEAD_SIZE)
            scores = lax.dot_general(
                heads, keys, (((1,), (1,)), ((), ())), preferred_element_type=F32
            ) * (1.0 / math.sqrt(HEAD_SIZE))
            masked = jnp.where(visible, scores, -1e30)
            highest = jnp.max(masked, axis=1, keepdims=True)
            expo = jnp.where(visible, jnp.exp(masked - highest), 0.0)
            probs = (expo / jnp.sum(expo, axis=1, keepdims=True)).astype(BF16)
            a_ref[t * half : (t + 1) * half, cols] = jnp.dot(
                probs, vals, preferred_element_type=F32
            ).astype(BF16)

    pl.semaphore_wait(barrier, mp - 1)

    @pl.loop(1, mp)
    def _(d):
        kv_copy(d).start()

    @pl.when(core == 0)
    def _():
        send_queries()

    own_q.wait()
    own_kv.wait()

    @pl.loop(1, mp)
    def _(d):
        kv_copy(d).wait_recv()

    kv_swap().start()
    attend(0)

    square[...] = jnp.zeros_like(square)
    acc[...] = jnp.zeros_like(acc)

    def multiply(u):
        t, j = u // n, lax.rem(u, n)

        @pl.when(t == 0)
        def _():
            w_copy(j, True).wait()

        lhs = a_ref[pl.ds(pl.multiple_of(t * half, half), half), :]
        res = jnp.dot(lhs, w[j, : lhs.shape[1], :], preferred_element_type=F32).astype(BF16)
        part[u, 0] = res[:, :hw]
        part[u, 1] = res[:, hw:]

        @pl.when(t == core)
        def _():
            for c in range(2):
                mine = part[u, c, span(own, tok), :].astype(F32) + res_ref[:, half_columns(j, c)].astype(F32)
                part[u, c, span(own, tok), :] = mine.astype(BF16)

        core_copy(u).start()

        @pl.when(t == 1)
        def _():
            w_copy(j, False).start()

    def add_core(u):
        core_copy(u).wait_recv()
        part[u, core] = (part[u, core].astype(F32) + from_core[u].astype(F32)).astype(BF16)
        one_copy(u).start()

    def add_one(u):
        b1, _, _, _ = order(lax.rem(u, n), TURN)
        one_copy(u).wait_recv()
        at = span(b1 * r1, r1)
        part[u, core, at, :] = (part[u, core, at, :].astype(F32) + from_one[u].astype(F32)).astype(BF16)
        two_copy(u).start()

    def add_two(u):
        b1, b2, _, _ = order(lax.rem(u, n), TURN)
        two_copy(u).wait_recv()
        at = span(b1 * r1 + b2 * r2, r2)
        part[u, core, at, :] = (part[u, core, at, :].astype(F32) + from_two[u].astype(F32)).astype(BF16)
        z_copy(u, 0).start()

    def add_z(u, k):
        b1, b2, _, _ = order(lax.rem(u, n), TURN)
        at = span(b1 * r1 + b2 * r2, r2)
        z_copy(u, k).wait_recv()
        total = (part[u, core, at, :].astype(F32) + from_z[u, k].astype(F32)).astype(BF16)
        if k < bits - 1:
            z_copy(u, k).wait_send()
            part[u, core, at, :] = total
            z_copy(u, k + 1).start()
        else:
            whole[u, core, at, :] = total
            gtwo_copy(u).start()

    def spread_one(u):
        gtwo_copy(u).wait_recv()
        gone_copy(u).start()

    def spread_core(u):
        gone_copy(u).wait_recv()
        gc_copy(u).start()

    def consume(u):
        t, j = u // n, lax.rem(u, n)
        gc_copy(u).wait_recv()

        @pl.when(t == 0)
        def _():
            gate_copy(j).wait()
            up_copy(j).wait()

        @pl.when(t == core)
        def _():
            for c in range(2):
                stream_ref[:, half_columns(j, c)] = whole[u, c, span(own, tok), :]

        total = square[...]
        for c in range(2):
            x = whole[u, c].astype(F32)
            for k in range(0, hw, 128):
                total += x[:, k : k + 128] * x[:, k : k + 128]
            for f in range(gained.shape[0]):
                gained[f, :, c * hw : (c + 1) * hw] = (x * gain_ref[f : f + 1, half_columns(j, c)]).astype(BF16)
        square[...] = total
        for s in range(slices):
            cols = slice(s * SLICE, (s + 1) * SLICE)
            both = jnp.concatenate([gate[j, :, cols], up[j, :, cols]], axis=1)
            acc[s] += jnp.dot(gained[table[me * slices + s]], both, preferred_element_type=F32)

        @pl.when(j == n - 1)
        def _():
            inv = lax.rsqrt(jnp.sum(square[...], axis=1, keepdims=True) / (n * cw) + 1e-05)
            for s in range(slices):
                both = acc[s] * inv
                g, u_ = both[:, :SLICE], both[:, SLICE:]
                hidden[t, :, s * SLICE : (s + 1) * SLICE] = (g / (1.0 + jnp.exp(-g)) * u_).astype(BF16)
            square[...] = jnp.zeros_like(square)
            acc[...] = jnp.zeros_like(acc)

    def multiply_down(u):
        t, j = u // n, lax.rem(u, n)
        core_copy(u).wait_send()
        one_copy(u).wait_send()
        two_copy(u).wait_send()
        z_copy(u, bits - 1).wait_send()

        @pl.when(t == 0)
        def _():
            w_copy(j, False).wait()

        lhs = hidden[t]
        res = jnp.dot(lhs, w[j, : lhs.shape[1], :], preferred_element_type=F32).astype(BF16)
        other = turned(j)
        for a in range(2):
            for b in range(2):
                at = span((a * 2 + b + other * (b - a)) * r2, r2)
                for c in range(2):
                    part[u, c, at, :] = res[(a * 2 + b) * r2 : (a * 2 + b + 1) * r2, c * hw : (c + 1) * hw]

        @pl.when(t != core)
        def _():
            own_core_copy(u).start()

    def mine_only(stage):
        def body(u):
            @pl.when(u // n == core)
            def _():
                stage(u)
        return body

    def own_add_core(u):
        j = lax.rem(u, n)
        own_core_copy(u).wait_recv()
        part[u] = (part[u].astype(F32) + own_core[j].astype(F32)).astype(BF16)
        own_one_copy(u).start()

    def own_add_one(u):
        j = lax.rem(u, n)
        b1, _, _, _ = order(j)
        own_one_copy(u).wait_recv()
        at = span(b1 * r1, r1)
        part[u, :, at, :] = (part[u, :, at, :].astype(F32) + own_one[j].astype(F32)).astype(BF16)
        own_two_copy(u).start()

    def own_add_two(u):
        j = lax.rem(u, n)
        own_two_copy(u).wait_recv()
        at = span(z_start(j, 0), r2)
        part[u, :, at, :] = (part[u, :, at, :].astype(F32) + own_two[j].astype(F32)).astype(BF16)
        own_z_copy(u, 0).start()

    def own_add_z(u, k):
        j = lax.rem(u, n)
        size = r2 >> (k + 1)
        own_z_copy(u, k).wait_recv()
        at = span(z_start(j, k + 1), size)
        total = part[u, :, at, :].astype(F32) + own_z[j, k, :, :size].astype(F32)
        if k < bits - 1:
            part[u, :, at, :] = total.astype(BF16)
            own_z_copy(u, k + 1).start()
        else:
            for c in range(2):
                cols = half_columns(j, c)
                mixed_ref[:, cols] = (stream_ref[:, cols].astype(F32) + total[c]).astype(BF16)

    def run(stages, last):
        @pl.loop(0, last)
        def _(i):
            @pl.when(i == SECOND)
            def _():
                attend(1)

            for lag, stage in stages:
                @pl.when((i >= lag) & (i < 2 * n + lag))
                def _(stage=stage, lag=lag):
                    stage(i - lag)

    first = [(0, multiply)]
    lag = 0
    for gap, stage in zip(GAPS, [add_core, add_one, add_two]):
        lag += gap
        first.append((lag, stage))
    for k in range(bits):
        lag += GAPS[3]
        first.append((lag, functools.partial(add_z, k=k)))
    for gap, stage in zip(GAPS[4:], [spread_one, spread_core, consume]):
        lag += gap
        first.append((lag, stage))
    lag += n
    second = [(lag, multiply_down)]
    for gap, stage in zip(OWN_GAPS, [own_add_core, own_add_one, own_add_two]):
        lag += gap
        second.append((lag, mine_only(stage)))
    for k in range(bits):
        lag += OWN_GAPS[3]
        second.append((lag, mine_only(functools.partial(own_add_z, k=k))))
    run((first + second)[::-1], 2 * n + lag)

    @pl.loop(1, mp)
    def _(d):
        kv_copy(d).wait_send()
        q_copy(d).wait_send()

    kv_swap().wait_send()

    @pl.loop(0, 2 * n)
    def _(u):
        gtwo_copy(u).wait_send()
        gone_copy(u).wait_send()
        gc_copy(u).wait_send()

        @pl.when(u // n != core)
        def _():
            own_core_copy(u).wait_send()

        @pl.when(u // n == core)
        def _():
            own_one_copy(u).wait_send()
            own_two_copy(u).wait_send()
            for k in range(bits):
                own_z_copy(u, k).wait_send()


def layer(seq_lens, table, queries, keys, vals, tokens, gain, out_weight, gate_weight, up_weight,
          down_weight, zs):
    tok, width = tokens.shape
    depth = out_weight.shape[0]
    mp = 4 * zs
    rows = tok * mp
    assert tok & (tok - 1) == 0 and zs & (zs - 1) == 0 and zs >= 4
    units = down_weight.shape[0]
    slices = units // SLICE
    n, cw, half = CHUNKS, width // CHUNKS, rows // 2
    hw = cw // 2
    bits = zs.bit_length() - 2
    dma = pltpu.SemaphoreType.DMA
    vmem = pl.BlockSpec(memory_space=pltpu.VMEM)
    hbm = pl.BlockSpec(memory_space=pl.ANY)
    m = 2 * n
    return pl.pallas_call(
        functools.partial(layer_kernel, zs, slices),
        out_shape=jax.ShapeDtypeStruct((2, tok, width), BF16),
        in_specs=[pl.BlockSpec(memory_space=pltpu.SMEM)] * 2 + [vmem] * 5 + [hbm] * 4,
        out_specs=vmem,
        scratch_shapes=[
            pltpu.VMEM((mp, tok, HEAD_SIZE), BF16),
            pltpu.VMEM((2, 2, zs, tok, depth), BF16),
            pltpu.VMEM((2, 2, 2, zs, tok, HEAD_SIZE), BF16),
            pltpu.VMEM((rows, depth), BF16),
            dma((mp,)), dma((mp,)), dma((mp,)), dma((mp,)), dma((1,)), dma((1,)), dma((2,)),
            pltpu.VMEM((n, max(depth, units), cw), BF16),
            pltpu.VMEM((n, cw, units), BF16),
            pltpu.VMEM((n, cw, units), BF16),
            pltpu.VMEM((m, 2, half, hw), BF16),
            pltpu.VMEM((m, 2, half, hw), BF16),
            pltpu.VMEM((m, half, hw), BF16),
            pltpu.VMEM((m, half // 2, hw), BF16),
            pltpu.VMEM((m, half // 4, hw), BF16),
            pltpu.VMEM((m, bits, half // 4, hw), BF16),
            pltpu.VMEM((n, 2, half, hw), BF16),
            pltpu.VMEM((n, 2, half // 2, hw), BF16),
            pltpu.VMEM((n, 2, half // 4, hw), BF16),
            pltpu.VMEM((n, bits, 2, half // 8, hw), BF16),
            pltpu.VMEM((gain.shape[0], half, cw), BF16),
            pltpu.VMEM((half, 128), F32),
            pltpu.VMEM((slices, half, 2 * SLICE), F32),
            pltpu.VMEM((2, half, units), BF16),
            dma((n,)), dma((n,)), dma((n,)),
            dma((m,)), dma((m,)), dma((m,)), dma((m,)), dma((m,)), dma((m,)), dma((m, bits)), dma((m, bits)),
            dma((m,)), dma((m,)), dma((m,)), dma((m,)), dma((m,)), dma((m,)),
            dma((n,)), dma((n,)), dma((n,)), dma((n,)), dma((n,)), dma((n,)), dma((n, bits)), dma((n, bits)),
        ],
        compiler_params=pltpu.CompilerParams(
            collective_id=0, has_side_effects=True, vmem_limit_bytes=62 << 20
        ),
        name="layer",
    )(seq_lens, table, queries, keys, vals, tokens, gain, out_weight, gate_weight, up_weight, down_weight)


def local(tokens, queries, key_proj, values, seq_lens, out_weight, ffn_gain, gate_weight, up_weight,
          down_weight, slice_table):
    both = layer(
        seq_lens, slice_table, queries, key_proj, values, tokens, ffn_gain, out_weight, gate_weight,
        up_weight, down_weight, lax.axis_size("mp") // 4
    )
    stream, mixed = both[0], both[1]
    return (stream, mixed)


def solution(mesh):
    placed = (
        P(("groups", "mp"), None),
        P(("groups", "mp"), None),
        P(("groups", "mp"), None),
        P(("groups", "mp"), None),
        P("groups"),
        P("mp", None),
        P(),
        P(None, "mp"),
        P(None, "mp"),
        P("mp", None),
        P(),
    )
    return jax.shard_map(
        local,
        mesh=mesh,
        in_specs=placed,
        out_specs=(P(("groups", "mp"), None), P(("groups", "mp"), None)),
        check_vma=False,
    )
```
